128 devices in a mesh: span: 8 (over z, core), xs: 16 (over y, x).
Axes of the slice: x: 4, y: 4, z: 4, core: 2. Of those that a mesh axis runs over, the one named last changes fastest.
Arguments:
- source: float32 [64, 64, 4096], P(None, 'span', 'xs'), may hold values from -0.75 to 0.75
- coefficient: float32 [64, 64, 4096], P(None, 'span', 'xs'), may hold values from 2.5 to 5
- volume_matrix: float32 [64, 64], replicated, may hold values from -0.75 to 0.75
- span_lower: float32 [64, 64], replicated, may hold values from -0.375 to 0.375
- span_upper: float32 [64, 64], replicated, may hold values from -0.375 to 0.375
- cross_lower: float32 [64, 64], replicated, may hold values from -0.375 to 0.375
- cross_upper: float32 [64, 64], replicated, may hold values from -0.375 to 0.375
- interface: int32 [8, 16, 128], P('span', 'xs'), may hold values from 0 to 131071
- compliance: float32 [8, 2048, 2048], P('span', 'xs'), may hold values from -0.5 to 0.5
- start_displacement: float32 [8, 16, 128], P('span', 'xs'), may hold values from -8 to 8
Outputs:
- fluid_state: float32 [64, 64, 4096], P(None, 'span', 'xs')
- shell_displacement: float32 [8, 16, 128], P('span', 'xs')
The draws below stay inside these ranges and needn't reach their ends.
All inputs are finite; a program needn't handle non-finite values.
Results may differ from the reference program's by a relative error of at most 0.0001.
Values sent between devices are 32-bit elements; how exact they have to be, the bound alone decides.
No kernel may reach another device: no remote copies, remote signals or barrier semaphores. Data moves between devices by JAX's collectives and lax.ppermute only.
A program may use at most 64 MiB of HBM per device.

```python
import jax
import jax.numpy as jnp
from jax import lax

NODES = 64
ES_DEV = 8
EX_DEV = 256
IF_DEV = 128
SUBITERS = 2
KRYLOV = 2
NS = 64
NX = 4096
SPANS = 8
GROUPS = 16
SHELL = 2048
N_SPAN = 8
N_XS = 16


def group_levels(key):
    return jax.random.bernoulli(jax.random.fold_in(key, 7), 0.5, (SPANS, GROUPS))


def draw_coefficient(key, part):
    lowered = group_levels(key)
    spread = jnp.repeat(jnp.repeat(lowered, ES_DEV, axis=0), EX_DEV, axis=1)
    parity = (jnp.arange(NX) % 2).astype(jnp.float32)[None, None, :]
    jitter = 0.3 * jax.random.uniform(jax.random.fold_in(key, 11), (NODES, NS, NX), jnp.float32)
    low_value = 2.5 + 0.6 * parity + jitter
    high_value = 4.1 + 0.6 * (1.0 - parity) + jitter
    return jnp.where(spread[None, :, :], low_value, high_value).astype(jnp.float32)


def draw_start_displacement(key, part):
    lowered = group_levels(key)
    values = 2.0 * jnp.clip(jax.random.normal(jax.random.fold_in(key, 13), (SPANS, GROUPS, IF_DEV), jnp.float32), -3.5, 3.5)
    return jnp.where(lowered[:, :, None], values, 0.0).astype(jnp.float32)


def set_ends(drawn, stream_key, least, top_value):
    longest = drawn.shape.index(max(drawn.shape))
    spots = []
    for shift in (0, 1):
        where = [jax.random.randint(jax.random.fold_in(stream_key, axis), (), 0, length) for axis, length in enumerate(drawn.shape)]
        where[longest] = (where[longest] + shift) % drawn.shape[longest]
        spots.append(tuple(where))
    return drawn.at[spots[0]].set(least).at[spots[1]].set(top_value)


def levels(own_key, extent, cuts, low, largest):
    loudness, own = 1.0, jax.random.fold_in(own_key, 6)
    for dim, parts in cuts:
        draws = jnp.exp(jax.random.uniform(jax.random.fold_in(own, dim), (parts,), jnp.float32, low / len(cuts), largest / len(cuts)))
        loudness = loudness * jnp.repeat(draws, extent[dim] // parts).reshape([-1 if axis == dim else 1 for axis in range(len(extent))])
    return loudness


def centred(key, extent, width, limit, cuts=(), held_as=jnp.bfloat16):
    values = jax.random.normal(key, extent, jnp.float32) * width
    if len(cuts) > 0:
        values = levels(key, extent, cuts, -0.22, 0.18) * values
    return jnp.clip(values, min=-limit, max=limit).astype(held_as)


def setup_inputs(seed: int = 0) -> dict:
    splits = jax.random.split(jax.random.key(seed), 11)
    source = centred(splits[0], (NODES, NS, NX), 0.05, 0.75, ((1, 8), (2, 16)), jnp.float32)
    coefficient = draw_coefficient(jax.random.fold_in(splits[10], 71), 0)
    volume_matrix = centred(splits[2], (NODES, NODES), NODES ** -0.5, 0.75, (), jnp.float32)
    span_lower = centred(splits[3], (NODES, NODES), (4 * NODES) ** -0.5, 0.375, (), jnp.float32)
    span_upper = centred(splits[4], (NODES, NODES), (4 * NODES) ** -0.5, 0.375, (), jnp.float32)
    cross_lower = centred(splits[5], (NODES, NODES), (4 * NODES) ** -0.5, 0.375, (), jnp.float32)
    cross_upper = centred(splits[6], (NODES, NODES), (4 * NODES) ** -0.5, 0.375, (), jnp.float32)
    interface = set_ends(jax.random.randint(splits[7], (SPANS, GROUPS, IF_DEV), 0, NODES * ES_DEV * EX_DEV), jax.random.fold_in(splits[7], 1), 0, (NODES * ES_DEV * EX_DEV) - 1).astype(jnp.int32)
    compliance = centred(splits[8], (SPANS, SHELL, SHELL), (SHELL // 16) ** -0.5, 0.5, ((0, 8), (1, 16)), jnp.float32)
    start_displacement = draw_start_displacement(jax.random.fold_in(splits[10], 71), 0)
    return dict(source=source, coefficient=coefficient, volume_matrix=volume_matrix, span_lower=span_lower, span_upper=span_upper, cross_lower=cross_lower, cross_upper=cross_upper, interface=interface, compliance=compliance, start_displacement=start_displacement)


exact_mode = lax.Precision.HIGHEST

def node_product(matrix, field):
    return jnp.einsum('ab,bsx->asx', matrix, field, precision=exact_mode)

def operate(field, coefficient, mats):
    volume_matrix, span_lower, span_upper, cross_lower, cross_upper = mats
    below = jnp.roll(field, 1, axis=1)
    above = jnp.roll(field, -1, axis=1)
    padded = jnp.pad(field, ((0, 0), (0, 0), (1, 1)))
    left = padded[:, :, :-2]
    right = padded[:, :, 2:]
    result = coefficient * field + node_product(volume_matrix, field)
    result = result - node_product(span_lower, below) - node_product(span_upper, above)
    return result - node_product(cross_lower, left) - node_product(cross_upper, right)

def to_groups(field):
    shaped = field.reshape(NODES, N_SPAN, ES_DEV, N_XS, EX_DEV)
    return shaped.transpose(1, 3, 0, 2, 4).reshape(N_SPAN, N_XS, NODES * ES_DEV * EX_DEV)

def from_groups(blocks):
    shaped = blocks.reshape(N_SPAN, N_XS, NODES, ES_DEV, EX_DEV)
    return shaped.transpose(2, 0, 3, 1, 4).reshape(NODES, N_SPAN * ES_DEV, N_XS * EX_DEV)

def place_one(indices, values):
    return jnp.zeros((NODES * ES_DEV * EX_DEV,), jnp.float32).at[indices].add(values)

def gmres(rhs, coefficient, mats):
    start_norm = jnp.sqrt(jnp.sum(rhs * rhs))
    basis = [rhs / start_norm]
    columns = []
    for step in range(KRYLOV):
        image = operate(basis[-1], coefficient, mats)
        project = jnp.stack([jnp.sum(vector * image) for vector in basis])
        for index in range(step + 1):
            image = image - project[index] * basis[index]
        length = jnp.sqrt(jnp.sum(image * image))
        columns.append(jnp.concatenate([project, length[None], jnp.zeros((KRYLOV - step - 1,), jnp.float32)]))
        basis.append(image / length)
    hessen = jnp.stack(columns, axis=1)
    gram = jnp.dot(hessen.T, hessen, precision=exact_mode)
    target = start_norm * hessen[0]
    factor = jnp.linalg.cholesky(gram)
    coeffs = jax.scipy.linalg.cho_solve((factor, True), target)
    result = coeffs[0] * basis[0]
    for index in range(1, KRYLOV):
        result = result + coeffs[index] * basis[index]
    return result

def reference(source, coefficient, volume_matrix, span_lower, span_upper, cross_lower, cross_upper, interface, compliance, start_displacement):
    mats = (volume_matrix, span_lower, span_upper, cross_lower, cross_upper)
    displacement = start_displacement
    fluid = source
    for sub in range(SUBITERS):
        forcing = jax.vmap(jax.vmap(place_one))(interface, displacement)
        rhs = source + from_groups(forcing)
        fluid = gmres(rhs, coefficient, mats)
        traces = jnp.take_along_axis(to_groups(fluid), interface, axis=2)
        fresh = jnp.einsum('sij,sj->si', compliance, traces.reshape(N_SPAN, N_XS * IF_DEV), precision=exact_mode)
        displacement = 0.5 * fresh.reshape(N_SPAN, N_XS, IF_DEV) + 0.5 * displacement
    return (fluid, displacement)
```

```python
import jax
import jax.numpy as jnp
from jax import lax
from jax.experimental import pallas as pl
from jax.experimental.pallas import tpu as pltpu
from jax.sharding import PartitionSpec as P

NODES, ES, EX, IFN = 64, 8, 256, 128
LANES = EX + 128
AXES = ("span", "xs")
THETA = 3.75
f32 = jnp.float32
bf16 = jnp.bfloat16
NT = (((1,), (1,)), ((), ()))


def parts(x):
    hi = x.astype(bf16)
    return hi, (x - hi.astype(f32)).astype(bf16)


def place(i):
    i = i.astype(jnp.int32)
    return i >> 11, (i >> 8) & 7, i & 255


def onehot(pos, size):
    rows = lax.broadcasted_iota(jnp.int32, (size, IFN), 0)
    return rows == pos


def pick(mask):
    return jnp.where(mask, 1.0, 0.0).astype(bf16)


def lane_rows(entries):
    rows = lax.broadcasted_iota(jnp.int32, (128, 128), 0)
    tile = jnp.zeros((128, 128), f32)
    for pos, value in entries:
        tile = jnp.where(rows == pos, value, tile)
    return tile.T


def fluid_kernel(
    src, cf, below, above, left, right, own, dmid, dbel, dabv, mats, mask,
    msg, *rest,
):
    *kept, r_scr, v_scr, l_scr = rest
    i_mid = (left[12:13], own[0:1], right[12:13])
    i_bel = (below[192:193, 128:], below[193:194, :128], below[193:194, 128:])
    i_abv = (above[192:193, 128:], above[193:194, :128], above[193:194, 128:])

    def forcing(idx, disp, shift, size):
        spots = [place(i) for i in idx]
        rows = [onehot((s + shift) * NODES + n, size) for n, s, _ in spots]
        d = [disp[k : k + 1] for k in range(3)]
        x = spots[1][2]
        sel = pick(rows[1])
        cols = parts(jnp.where(onehot(x, EX), d[1], 0.0))
        body = lax.dot_general(
            jnp.concatenate([sel, sel], 1), jnp.concatenate(cols, 1), NT,
            preferred_element_type=f32,
        )
        xl, xr = spots[0][2], spots[2][2]
        cl = parts(jnp.where(onehot(jnp.where(xl >= EX - 2, xl - 128, -1), 128), d[0], 0.0))
        cr = parts(jnp.where(onehot(jnp.where(xr < 2, xr, -1), 128), d[2], 0.0))
        sl, sr = pick(rows[0]), pick(rows[2])
        side = lax.dot_general(
            jnp.concatenate([sl, sl, sr, sr], 1), jnp.concatenate(cl + cr, 1), NT,
            preferred_element_type=f32,
        )
        return body, side, rows[1], x

    body, side, row_mask, x_own = forcing(i_mid, dmid, 0, ES * NODES)
    for s in range(ES):
        at = slice((s + 2) * NODES, (s + 3) * NODES)
        r_scr[at, :EX] = src[s * NODES : (s + 1) * NODES, :] + body[s * NODES : (s + 1) * NODES]
    for p in range(4):
        at = slice((2 * p + 2) * NODES, (2 * p + 4) * NODES)
        tile = lane_rows(
            ((0, right[p : p + 1]), (1, right[4 + p : 5 + p]), (126, left[p : p + 1]), (127, left[4 + p : 5 + p]))
        )
        r_scr[at, EX:] = tile + side[2 * p * NODES : (2 * p + 2) * NODES]
        l_scr[at, :] = lane_rows(((0, right[8 + p : 9 + p]), (127, left[8 + p : 9 + p])))
    cb, ct = below[192:193, :128], above[192:193, :128]
    half = lax.broadcasted_iota(jnp.int32, (1, 128), 1) < NODES
    corner = lane_rows(
        (
            (0, jnp.where(half, pltpu.roll(cb, NODES, 1), ct)),
            (127, jnp.where(half, cb, pltpu.roll(ct, NODES, 1))),
        )
    )
    body, side, _, _ = forcing(i_bel, dbel, 2 - ES, 2 * NODES)
    r_scr[: 2 * NODES, :EX] = below[: 2 * NODES] + body
    r_scr[: 2 * NODES, EX:] = side
    r_scr[NODES : 2 * NODES, EX:] += corner[:NODES]
    body, side, _, _ = forcing(i_abv, dabv, 0, 2 * NODES)
    r_scr[10 * NODES :, :EX] = above[: 2 * NODES] + body
    r_scr[10 * NODES :, EX:] = side
    r_scr[10 * NODES : 11 * NODES, EX:] += corner[NODES:]

    def product(ref, s, lo, hi):
        x = ref[s * NODES : (s + 1) * NODES, :]
        xh, xl = parts(x)
        return jnp.dot(
            mats[lo * NODES : hi * NODES, :], jnp.concatenate([xh, xh, xl], 0),
            preferred_element_type=f32,
        )

    def base(prod):
        return (
            prod[:NODES]
            + pltpu.roll(prod[3 * NODES : 4 * NODES], 1, 1)
            + pltpu.roll(prod[4 * NODES :], LANES - 1, 1)
        )

    def coef(s):
        if s == 1:
            return jnp.concatenate([below[2 * NODES : 3 * NODES], jnp.zeros((NODES, 128), f32)], 1)
        if s == 10:
            return jnp.concatenate([above[2 * NODES : 3 * NODES], jnp.zeros((NODES, 128), f32)], 1)
        return jnp.concatenate(
            [cf[(s - 2) * NODES : (s - 1) * NODES, :], l_scr[s * NODES : (s + 1) * NODES, :]], 1
        )

    keep = mask[0:1, :]
    low = product(r_scr, 0, 1, 2)
    pending = None
    for s in range(1, 12):
        if s < 11:
            prod = product(r_scr, s, 0, 5)
            up = prod[2 * NODES : 3 * NODES]
        else:
            up = product(r_scr, s, 2, 3)
        if pending is not None:
            v_scr[(s - 1) * NODES : s * NODES, :] = (pending + up) * keep
        if s < 11:
            pending = coef(s) * r_scr[s * NODES : (s + 1) * NODES, :] + base(prod) + low
            low = prod[NODES : 2 * NODES]

    sums = [jnp.zeros((8, EX), f32) for _ in range(5)]
    low = product(v_scr, 1, 1, 2)[:, :EX]
    pending = None
    for s in range(2, 11):
        if s < 10:
            prod = product(v_scr, s, 0, 5)
            up = prod[2 * NODES : 3 * NODES, :EX]
        else:
            up = product(v_scr, s, 2, 3)[:, :EX]
        if pending is not None:
            at = slice((s - 1) * NODES, s * NODES)
            r, v = r_scr[at, :EX], v_scr[at, :EX]
            w = pending + up - THETA * v
            pairs = ((v, v), (v, w), (w, w), (r, v), (r, w))
            for k, (a, b) in enumerate(pairs):
                sums[k] = sums[k] + jnp.sum((a * b).reshape(8, 8, EX), axis=0)
        if s < 10:
            at = slice(s * NODES, (s + 1) * NODES)
            pending = cf[(s - 2) * NODES : (s - 1) * NODES, :] * v_scr[at, :EX] + base(prod)[:, :EX] + low
            low = prod[NODES : 2 * NODES, :EX]

    lane = lax.broadcasted_iota(jnp.int32, (1, 128), 1)
    gram = jnp.zeros((1, 128), f32)
    for k in range(5):
        total = jnp.sum(jnp.sum(sums[k], axis=0, keepdims=True), axis=1, keepdims=True)
        gram = gram + jnp.where(lane == k, total, 0.0)
    cols = pick(onehot(x_own, EX))
    cols = jnp.concatenate([cols, cols], 0)
    rows = [gram]
    for ref in (r_scr, v_scr):
        hi, lo = parts(ref[2 * NODES : 10 * NODES, :EX])
        found = jnp.dot(jnp.concatenate([hi, lo], 1), cols, preferred_element_type=f32)
        rows.append(jnp.sum(jnp.where(row_mask, found, 0.0), axis=0, keepdims=True))
    msg[...] = jnp.broadcast_to(jnp.concatenate(rows, 1), msg.shape)
    if kept:
        kept[0][...] = r_scr[2 * NODES : 10 * NODES, :EX]
        kept[1][...] = v_scr[2 * NODES : 10 * NODES, :EX]


def solve(got):
    total = jnp.sum(got[:, :128], axis=0, keepdims=True)
    lane = lax.broadcasted_iota(jnp.int32, (1, 128), 1)
    g11, g12, g22, g1, g2 = (
        jnp.sum(jnp.where(lane == k, total, 0.0), axis=1, keepdims=True) for k in range(5)
    )
    ratio = g12 / g11
    b = (g2 - ratio * g1) / (g22 - ratio * g12)
    a = (g1 - b * g12) / g11
    return a - THETA * b, b


def shell_kernel(section, got, compliance, disp, *rest):
    if len(rest) > 1:
        r, v, fluid, out = rest
    else:
        (out,) = rest
    a, b = solve(got)
    start = pl.multiple_of(section[0] * 16, 16)
    traces = a * got[pl.ds(start, 16), 128:256] + b * got[pl.ds(start, 16), 256:]
    acc = jnp.zeros((IFN, 128), f32)
    for j in range(16):
        acc = acc + compliance[:, j * 128 : (j + 1) * 128] * traces[j : j + 1]
    fresh = jnp.sum(acc.T, axis=0, keepdims=True)
    out[...] = 0.5 * fresh + 0.5 * disp[0:1]
    if len(rest) > 1:
        for s in range(ES):
            at = slice(s * NODES, (s + 1) * NODES)
            fluid[:, s, :] = a * r[at, :] + b * v[at, :]


def columns(field, lo, hi):
    return jnp.transpose(field[:, :, lo:hi], (2, 1, 0)).reshape(-1, 128)


def layers(field, lo, hi):
    return jnp.transpose(field[:, lo:hi, :], (1, 0, 2)).reshape(-1, EX)


def body(
    source, coefficient, volume_matrix, span_lower, span_upper, cross_lower,
    cross_upper, interface, compliance, start_displacement,
):
    n_span, n_xs = lax.axis_size("span"), lax.axis_size("xs")
    up = [(i, i + 1) for i in range(n_xs - 1)]
    down = [(i + 1, i) for i in range(n_xs - 1)]
    fore = [(i, (i + 1) % n_span) for i in range(n_span)]
    back = [((i + 1) % n_span, i) for i in range(n_span)]
    disp = start_displacement[0]
    own = interface[0].astype(f32)
    tail = [own, disp, jnp.zeros((2, 128), f32)]
    left = lax.ppermute(
        jnp.concatenate([columns(source, EX - 2, EX), columns(coefficient, EX - 1, EX)] + tail), "xs", up
    )
    right = lax.ppermute(
        jnp.concatenate([columns(source, 0, 2), columns(coefficient, 0, 1)] + tail), "xs", down
    )
    stacked = jnp.concatenate(
        [volume_matrix, -span_lower, -span_upper, -cross_lower, -cross_upper], 0
    )
    high = lax.reduce_precision(stacked, 8, 7)
    mats = jnp.concatenate([high, stacked - high, high], 1).astype(bf16)
    index = lax.axis_index("xs")
    lane = jnp.arange(LANES)
    inside = (lane < EX) | ((lane < EX + 2) & (index < n_xs - 1)) | ((lane >= LANES - 2) & (index > 0))
    mask = jnp.broadcast_to(jnp.where(inside, 1.0, 0.0).astype(f32)[None], (8, LANES))
    section = lax.axis_index("span").astype(jnp.int32)[None]

    def edge(first, corner_l, corner_r):
        corner = jnp.concatenate([corner_l, corner_r])[None]
        small = jnp.concatenate(
            [corner, left[12:13], own, right[12:13], left[13:14], disp, right[13:14]]
            + [jnp.zeros((9, 128), f32)]
        ).reshape(8, EX)
        inner = ES - 1 if first else 0
        both = layers(source, ES - 2, ES) if first else layers(source, 0, 2)
        return jnp.concatenate([both, layers(coefficient, inner, inner + 1), small])

    below = lax.ppermute(edge(True, left[7, NODES:], right[3, NODES:]), "span", fore)
    above = lax.ppermute(edge(False, left[4, :NODES], right[0, :NODES]), "span", back)

    src = layers(source, 0, ES)
    cf = layers(coefficient, 0, ES)

    def tails(edges):
        return edges[194:196].reshape(4, 128)[:3]

    def fluid_step(dmid, dbel, dabv, keep):
        shapes = [jax.ShapeDtypeStruct((128, 3 * 128), f32)]
        if keep:
            shapes += [jax.ShapeDtypeStruct((ES * NODES, EX), f32)] * 2
        return pl.pallas_call(
            fluid_kernel,
            out_shape=shapes,
            scratch_shapes=[
                pltpu.VMEM((12 * NODES, LANES), f32),
                pltpu.VMEM((12 * NODES, LANES), f32),
                pltpu.VMEM((12 * NODES, 128), f32),
            ],
            name="fluid_keep" if keep else "fluid",
        )(src, cf, below, above, left, right, own, dmid, dbel, dabv, mats, mask)

    vm = pl.BlockSpec(memory_space=pltpu.VMEM)
    sm = pl.BlockSpec(memory_space=pltpu.SMEM)

    def exchange(message):
        return lax.all_to_all(message, AXES, 0, 0)

    rows = compliance[0]
    dmid = jnp.concatenate([left[13:14], disp, right[13:14]])
    (message,) = fluid_step(dmid, tails(below), tails(above), False)
    got = exchange(message)
    disp = pl.pallas_call(
        shell_kernel,
        out_shape=jax.ShapeDtypeStruct((1, 128), f32),
        in_specs=[sm, vm, vm, vm],
        out_specs=vm,
        name="shell",
    )(section, got, rows, disp)
    dl = lax.ppermute(disp, "xs", up)
    dr = lax.ppermute(disp, "xs", down)
    dmid = jnp.concatenate([dl, disp, dr])
    dbel = lax.ppermute(dmid, "span", fore)
    dabv = lax.ppermute(dmid, "span", back)
    message, r, v = fluid_step(dmid, dbel, dabv, True)
    got = exchange(message)
    fluid, disp = pl.pallas_call(
        shell_kernel,
        out_shape=[
            jax.ShapeDtypeStruct((NODES, ES, EX), f32),
            jax.ShapeDtypeStruct((1, 128), f32),
        ],
        in_specs=[sm, vm, vm, vm, vm, vm],
        out_specs=[vm, vm],
        name="shell_last",
    )(section, got, rows, disp, r, v)
    return fluid, disp[None]


def solution(mesh):
    field = P(None, "span", "xs")
    section = P("span", "xs", None)
    return jax.shard_map(
        body,
        mesh=mesh,
        in_specs=(field, field, P(), P(), P(), P(), P(), section, section, section),
        out_specs=(field, section),
        check_vma=False,
    )
```

```python
import jax
import jax.numpy as jnp
from jax import lax
from jax.experimental import pallas as pl
from jax.experimental.pallas import tpu as pltpu
from jax.sharding import PartitionSpec as P

NODES, ES, EX, IFN = 64, 8, 256, 128
LANES = EX + 128
AXES = ("span", "xs")
THETA = 3.75
f32 = jnp.float32
bf16 = jnp.bfloat16
NT = (((1,), (1,)), ((), ()))


def parts(x):
    hi = x.astype(bf16)
    return hi, (x - hi.astype(f32)).astype(bf16)


def place(i):
    i = i.astype(jnp.int32)
    return i >> 11, (i >> 8) & 7, i & 255


def onehot(pos, size):
    rows = lax.broadcasted_iota(jnp.int32, (size, IFN), 0)
    return rows == pos


def pick(mask):
    return jnp.where(mask, 1.0, 0.0).astype(bf16)


def lane_rows(entries):
    rows = lax.broadcasted_iota(jnp.int32, (128, 128), 0)
    tile = jnp.zeros((128, 128), f32)
    for pos, value in entries:
        tile = jnp.where(rows == pos, value, tile)
    return tile.T


def position():
    return lax.axis_index("span"), lax.axis_index("xs")


def pack_cross(src_hbm, cf_hbm, own_hbm, disp_hbm, first, second, own, disp, src, cf, scr, sems):
    pairs = ((src_hbm, src), (cf_hbm, cf), (own_hbm, own), (disp_hbm, disp))
    copies = [pltpu.make_async_copy(a, b, sems.at[k]) for k, (a, b) in enumerate(pairs)]
    for copy in copies:
        copy.start()
    for copy in copies:
        copy.wait()
    lane = lax.broadcasted_iota(jnp.int32, (2 * NODES, 128), 1)
    tile = jnp.zeros((2 * NODES, 128), f32)
    for p in range(4):
        for ref, wide, at in ((src, 2, 2 * p), (cf, 1, 8 + p)):
            both = jnp.concatenate([ref[:, 2 * p, :], ref[:, 2 * p + 1, :]], 0)
            high = pltpu.roll(both[:, 128:], at + wide, 1)
            low = pltpu.roll(both[:, :128], 64 + at, 1)
            tile = jnp.where((lane >= at) & (lane < at + wide), high, tile)
            tile = jnp.where((lane >= 64 + at) & (lane < 64 + at + wide), low, tile)
    scr[...] = tile.T
    odd = (position()[1] % 2) * 64
    for out, start in ((first, odd), (second, 64 - odd)):
        out[...] = scr[pl.ds(pl.multiple_of(start, 64), 16), :]
        out[12:13] = own[...].astype(f32)
        out[13:14] = disp[...]


def sides(index, first, second):
    even = index % 2 == 0
    return jnp.where(even, second, first), jnp.where(even, first, second)


def pack_span(src, cf, cross_a, cross_b, own, disp, first, second):
    where = position()
    half = lax.broadcasted_iota(jnp.int32, (1, 128), 1) < NODES
    mine = own[...].astype(f32)
    left, right = sides(where[1], cross_a[...], cross_b[...])
    even = where[0] % 2 == 0
    after = jnp.where(half, pltpu.roll(left[7:8], NODES, 1), right[6:7])
    before = jnp.where(half, left[1:2], pltpu.roll(right[0:1], NODES, 1))
    for out, top in ((first, even), (second, jnp.logical_not(even))):

        @pl.when(top)
        def _():
            out[:NODES] = src[:, ES - 2, :]
            out[NODES : 2 * NODES] = src[:, ES - 1, :]
            out[2 * NODES : 3 * NODES] = cf[:, ES - 1, :]

        @pl.when(jnp.logical_not(top))
        def _():
            out[:NODES] = src[:, 0, :]
            out[NODES : 2 * NODES] = src[:, 1, :]
            out[2 * NODES : 3 * NODES] = cf[:, 0, :]

        corner = jnp.where(top, after, before)
        out[192:193] = jnp.concatenate([corner, left[12:13]], 1)
        out[193:194] = jnp.concatenate([mine, right[12:13]], 1)
        out[194:195] = jnp.concatenate([left[13:14], disp[...]], 1)
        out[195:196] = jnp.concatenate([right[13:14], jnp.zeros((1, 128), f32)], 1)
        out[196:200] = jnp.zeros((4, EX), f32)


def join(cross_a, cross_b, d, out):
    dl, dr = sides(position()[1], cross_a[...], cross_b[...])
    out[...] = jnp.concatenate([dl, d[...], dr], 0)


def forcing(idx, disp, shift, size):
    spots = [place(i) for i in idx]
    rows = [onehot((s + shift) * NODES + n, size) for n, s, _ in spots]
    x = spots[1][2]
    sel = pick(rows[1])
    cols = parts(jnp.where(onehot(x, EX), disp[1], 0.0))
    main = lax.dot_general(
        jnp.concatenate([sel, sel], 1), jnp.concatenate(cols, 1), NT, preferred_element_type=f32
    )
    xl, xr = spots[0][2], spots[2][2]
    cl = parts(jnp.where(onehot(jnp.where(xl >= EX - 2, xl - 128, -1), 128), disp[0], 0.0))
    cr = parts(jnp.where(onehot(jnp.where(xr < 2, xr, -1), 128), disp[2], 0.0))
    sl, sr = pick(rows[0]), pick(rows[2])
    side = lax.dot_general(
        jnp.concatenate([sl, sl, sr, sr], 1), jnp.concatenate(cl + cr, 1), NT,
        preferred_element_type=f32,
    )
    return main, side, rows[1], x


def extend(src, cf, below, above, left, right, ext, edge):
    for s in range(ES):
        ext[(s + 2) * NODES : (s + 3) * NODES, :EX] = src[:, s, :]
    for p in range(4):
        at = slice((2 * p + 2) * NODES, (2 * p + 4) * NODES)
        k = 2 * p
        ext[at, EX:] = lane_rows(
            ((0, right[k : k + 1]), (1, right[k + 1 : k + 2]), (126, left[k : k + 1]), (127, left[k + 1 : k + 2]))
        )
        edge[at, :] = lane_rows(((0, right[8 + p : 9 + p]), (127, left[8 + p : 9 + p])))
    cb, ct = below[192:193, :128], above[192:193, :128]
    half = lax.broadcasted_iota(jnp.int32, (1, 128), 1) < NODES
    corner = lane_rows(
        (
            (0, jnp.where(half, pltpu.roll(cb, NODES, 1), ct)),
            (127, jnp.where(half, cb, pltpu.roll(ct, NODES, 1))),
        )
    )
    none = jnp.zeros((NODES, 128), f32)
    ext[: 2 * NODES, :EX] = below[: 2 * NODES]
    ext[: 2 * NODES, EX:] = jnp.concatenate([none, corner[:NODES]], 0)
    ext[10 * NODES :, :EX] = above[: 2 * NODES]
    ext[10 * NODES :, EX:] = jnp.concatenate([corner[NODES:], none], 0)


def fluid_kernel(first, n_xs, *refs):
    where = position()
    src, cf, span_a, span_b, cross_a, cross_b, own, *refs, below, above = refs
    below[...], above[...] = sides(where[0], span_a[...], span_b[...])
    left, right = sides(where[1], cross_a[...], cross_b[...])
    if first:
        disp, *raw, msg, ext, edge, mats, r_scr, v_scr = refs
        d_mid = (left[13:14], disp[...], right[13:14])
        d_bel = (below[194:195, :128], below[194:195, 128:], below[195:196, :128])
        d_abv = (above[194:195, :128], above[194:195, 128:], above[195:196, :128])
        extend(src, cf, below, above, left, right, ext, edge)
        for k, ref in enumerate(raw):
            m = ref[...] if k == 0 else -ref[...]
            high = m.astype(bf16).astype(f32)
            mats[k * NODES : (k + 1) * NODES, :] = jnp.concatenate([high, m - high, high], 1).astype(bf16)
    else:
        dmid, d_a, d_b, ext, edge, mats, msg, r_out, v_out, r_scr, v_scr = refs
        d_mid, d_bel, d_abv = (
            (d[0:1], d[1:2], d[2:3]) for d in (dmid[...], *sides(where[0], d_a[...], d_b[...]))
        )
    i_mid = (left[12:13], own[...], right[12:13])
    i_bel = (below[192:193, 128:], below[193:194, :128], below[193:194, 128:])
    i_abv = (above[192:193, 128:], above[193:194, :128], above[193:194, 128:])

    main, side, row_mask, x_own = forcing(i_mid, d_mid, 0, ES * NODES)
    mid = slice(2 * NODES, 10 * NODES)
    r_scr[mid, :EX] = ext[mid, :EX] + main
    r_scr[mid, EX:] = ext[mid, EX:] + side
    for idx, disp3, shift, at in (
        (i_bel, d_bel, 2 - ES, slice(0, 2 * NODES)),
        (i_abv, d_abv, 0, slice(10 * NODES, 12 * NODES)),
    ):
        main, side, _, _ = forcing(idx, disp3, shift, 2 * NODES)
        r_scr[at, :EX] = ext[at, :EX] + main
        r_scr[at, EX:] = ext[at, EX:] + side

    def product(ref, s, lo, hi):
        x = ref[s * NODES : (s + 1) * NODES, :]
        xh, xl = parts(x)
        return jnp.dot(
            mats[lo * NODES : hi * NODES, :], jnp.concatenate([xh, xh, xl], 0),
            preferred_element_type=f32,
        )

    def base(prod):
        return (
            prod[:NODES]
            + pltpu.roll(prod[3 * NODES : 4 * NODES], 1, 1)
            + pltpu.roll(prod[4 * NODES :], LANES - 1, 1)
        )

    def coef(s):
        if s == 1:
            return jnp.concatenate([below[2 * NODES : 3 * NODES], jnp.zeros((NODES, 128), f32)], 1)
        if s == 10:
            return jnp.concatenate([above[2 * NODES : 3 * NODES], jnp.zeros((NODES, 128), f32)], 1)
        return jnp.concatenate([cf[:, s - 2, :], edge[s * NODES : (s + 1) * NODES, :]], 1)

    lanes = lax.broadcasted_iota(jnp.int32, (1, LANES), 1)
    keep = jnp.where(
        (lanes < EX)
        | ((lanes < EX + 2) & (where[1] < n_xs - 1))
        | ((lanes >= LANES - 2) & (where[1] > 0)),
        1.0,
        0.0,
    ).astype(f32)
    low = product(r_scr, 0, 1, 2)
    pending = None
    for s in range(1, 12):
        if s < 11:
            prod = product(r_scr, s, 0, 5)
            up = prod[2 * NODES : 3 * NODES]
        else:
            up = product(r_scr, s, 2, 3)
        if pending is not None:
            v_scr[(s - 1) * NODES : s * NODES, :] = (pending + up) * keep
        if s < 11:
            pending = coef(s) * r_scr[s * NODES : (s + 1) * NODES, :] + base(prod) + low
            low = prod[NODES : 2 * NODES]

    sums = [jnp.zeros((8, EX), f32) for _ in range(5)]
    low = product(v_scr, 1, 1, 2)[:, :EX]
    pending = None
    for s in range(2, 11):
        if s < 10:
            prod = product(v_scr, s, 0, 5)
            up = prod[2 * NODES : 3 * NODES, :EX]
        else:
            up = product(v_scr, s, 2, 3)[:, :EX]
        if pending is not None:
            at = slice((s - 1) * NODES, s * NODES)
            r, v = r_scr[at, :EX], v_scr[at, :EX]
            w = pending + up - THETA * v
            pairs = ((v, v), (v, w), (w, w), (r, v), (r, w))
            for k, (a, b) in enumerate(pairs):
                sums[k] = sums[k] + jnp.sum((a * b).reshape(8, 8, EX), axis=0)
        if s < 10:
            at = slice(s * NODES, (s + 1) * NODES)
            pending = cf[:, s - 2, :] * v_scr[at, :EX] + base(prod)[:, :EX] + low
            low = prod[NODES : 2 * NODES, :EX]

    lane = lax.broadcasted_iota(jnp.int32, (1, 128), 1)
    gram = jnp.zeros((1, 128), f32)
    for k in range(5):
        total = jnp.sum(jnp.sum(sums[k], axis=0, keepdims=True), axis=1, keepdims=True)
        gram = gram + jnp.where(lane == k, total, 0.0)
    cols = pick(onehot(x_own, EX))
    cols = jnp.concatenate([cols, cols], 0)
    rows = [gram]
    for ref in (r_scr, v_scr):
        hi, lo = parts(ref[mid, :EX])
        found = jnp.dot(jnp.concatenate([hi, lo], 1), cols, preferred_element_type=f32)
        rows.append(jnp.sum(jnp.where(row_mask, found, 0.0), axis=0, keepdims=True))
    msg[...] = jnp.broadcast_to(jnp.concatenate(rows, 1)[None], msg.shape)
    if not first:
        r_out[...] = r_scr[mid, :EX]
        v_out[...] = v_scr[mid, :EX]


def solve(got):
    total = jnp.sum(got[:, 0, :128], axis=0, keepdims=True)
    lane = lax.broadcasted_iota(jnp.int32, (1, 128), 1)
    g11, g12, g22, g1, g2 = (
        jnp.sum(jnp.where(lane == k, total, 0.0), axis=1, keepdims=True) for k in range(5)
    )
    ratio = g12 / g11
    b = (g2 - ratio * g1) / (g22 - ratio * g12)
    a = (g1 - b * g12) / g11
    return a - THETA * b, b


def shell_kernel(got, compliance, disp, *rest):
    out = rest[-1]
    a, b = solve(got)
    start = position()[0] * 16
    traces = a * got[pl.ds(start, 16), 0, 128:256] + b * got[pl.ds(start, 16), 0, 256:]
    acc = jnp.zeros((IFN, 128), f32)
    for j in range(16):
        acc = acc + compliance[:, j * 128 : (j + 1) * 128] * traces[j : j + 1]
    fresh = jnp.sum(acc.T, axis=0, keepdims=True)
    out[...] = 0.5 * fresh + 0.5 * disp[...]
    if len(rest) > 1:
        r, v, fluid, _ = rest
        for s in range(ES):
            at = slice(s * NODES, (s + 1) * NODES)
            fluid[:, s, :] = a * r[at, :] + b * v[at, :]


def call(kernel, name, outs, ins, scratch=(), pinned=True):
    vm = pl.BlockSpec(memory_space=pltpu.VMEM)
    make = pltpu.VMEM if pinned else jax.ShapeDtypeStruct
    return pl.pallas_call(
        kernel,
        out_shape=[make(*o) for o in outs],
        in_specs=[vm] * len(ins),
        out_specs=[vm] * len(outs),
        scratch_shapes=[pltpu.VMEM(x, f32) for x in scratch],
        compiler_params=pltpu.CompilerParams(vmem_limit_bytes=16 << 20),
        name=name,
    )(*(pltpu.with_memory_space_constraint(x, pltpu.VMEM) for x in ins))


def swaps(axis, wrap):
    size = lax.axis_size(axis)
    pairs = [(i, i + 1) for i in range(size - 1)] + ([(size - 1, 0)] if wrap else [])
    return [[p for i, j in pairs[k::2] for p in ((i, j), (j, i))] for k in (0, 1)]


def body(
    source, coefficient, volume_matrix, span_lower, span_upper, cross_lower,
    cross_upper, interface, compliance, start_displacement,
):
    n_xs = lax.axis_size("xs")
    own, disp, rows = interface[0], start_displacement[0], compliance[0]
    mats = [volume_matrix, span_lower, span_upper, cross_lower, cross_upper]
    message, block = ((128, 1, 3 * 128), f32), ((ES * NODES, EX), f32)
    ext, edges = (12 * NODES, LANES), (200, EX)

    def trade(axis, a, b):
        first, second = swaps(axis, axis == "span")
        return [lax.ppermute(a, axis, first), lax.ppermute(b, axis, second)]

    args = [source, coefficient, own, disp]
    far = pl.BlockSpec(memory_space=pl.ANY)
    *packed, own, disp = pl.pallas_call(
        pack_cross,
        out_shape=[pltpu.VMEM((16, 128), f32)] * 2 + [pltpu.VMEM(x.shape, x.dtype) for x in args[2:]],
        in_specs=[far] * 4,
        out_specs=[pl.BlockSpec(memory_space=pltpu.VMEM)] * 4,
        scratch_shapes=[pltpu.VMEM(x.shape, x.dtype) for x in args[:2]]
        + [pltpu.VMEM((128, 128), f32), pltpu.SemaphoreType.DMA((4,))],
        compiler_params=pltpu.CompilerParams(vmem_limit_bytes=16 << 20),
        name="pack_cross",
    )(*(pltpu.with_memory_space_constraint(x, pltpu.HBM) for x in args))
    cross = trade("xs", *packed)
    packed = call(
        pack_span, "pack_span", [(edges, f32)] * 2, [source, coefficient, *cross, own, disp]
    )
    around = [source, coefficient, *trade("span", *packed), *cross, own]

    sent, base, edge, split = call(
        lambda *refs: fluid_kernel(True, n_xs, *refs), "fluid",
        [message, (ext, f32), ((12 * NODES, 128), f32), ((5 * NODES, 3 * NODES), bf16)],
        around + [disp] + mats, [ext, ext, edges, edges],
    )
    got = lax.all_to_all(sent, AXES, 0, 0, tiled=True)
    (disp,) = call(shell_kernel, "shell", [((1, 128), f32)], [got, rows, disp])
    (mid,) = call(join, "join", [((3, 128), f32)], [*trade("xs", disp, disp), disp])
    sent, r, v = call(
        lambda *refs: fluid_kernel(False, n_xs, *refs), "fluid_last", [message, block, block],
        around + [mid, *trade("span", mid, mid), base, edge, split], [ext, ext, edges, edges],
    )
    got = lax.all_to_all(sent, AXES, 0, 0, tiled=True)
    fluid, disp = call(
        shell_kernel, "shell_last", [(source.shape, f32), ((1, 128), f32)],
        [got, rows, disp, r, v], (), False,
    )
    return fluid, disp[None]


def solution(mesh):
    field = P(None, "span", "xs")
    section = P("span", "xs", None)
    return jax.shard_map(
        body,
        mesh=mesh,
        in_specs=(field, field, P(), P(), P(), P(), P(), section, section, section),
        out_specs=(field, section),
        check_vma=False,
    )
```

```python
import jax
import jax.numpy as jnp
from jax import lax
from jax.experimental import pallas as pl
from jax.experimental.pallas import tpu as pltpu
from jax.sharding import PartitionSpec as P


NODES, ES, EX, IFN = 64, 8, 256, 128
LANES = EX + 128
AXES = ("span", "xs")
THETA = 3.75
f32 = jnp.float32
bf16 = jnp.bfloat16
NT = (((1,), (1,)), ((), ()))


def parts(x):
    hi = x.astype(bf16)
    return hi, (x - hi.astype(f32)).astype(bf16)


def place(i):
    i = i.astype(jnp.int32)
    return i >> 11, (i >> 8) & 7, i & 255


def onehot(pos, size):
    rows = lax.broadcasted_iota(jnp.int32, (size, IFN), 0)
    return rows == pos


def pick(mask):
    return jnp.where(mask, 1.0, 0.0).astype(bf16)


def lane_rows(entries):
    rows = lax.broadcasted_iota(jnp.int32, (128, 128), 0)
    tile = jnp.zeros((128, 128), f32)
    for pos, value in entries:
        tile = jnp.where(rows == pos, value, tile)
    return tile.T


def at(s, first=0):
    return slice((s - first) * NODES, (s - first + 1) * NODES)


def position():
    return lax.axis_index("span"), lax.axis_index("xs")


def pack(*refs):
    far, (columns, edge_a, edge_b, *near, halves, sems) = refs[:9], refs[9:]
    src, cf, own, disp, *_ = near
    pairs = [(f.at[:, pl.ds(h * 128, 128)], halves.at[2 * k + h]) for k, f in enumerate(far[:2]) for h in (0, 1)]
    pairs += list(zip(far[2:], near[2:]))
    copies = [pltpu.make_async_copy(a, b, sems.at[k]) for k, (a, b) in enumerate(pairs)]
    for copy in copies:
        copy.start()
    lane = lax.broadcasted_iota(jnp.int32, (1, 128), 1)
    tile = jnp.zeros((2 * NODES, 128), f32)
    for k, (ref, wide, base) in enumerate(((src, 2, 0), (cf, 1, 16))):
        copies[2 * k].wait()
        copies[2 * k + 1].wait()
        for p in range(4):
            slot = base + 2 * wide * p
            low, high = (
                jnp.concatenate([halves[2 * k + h, pl.ds(2 * p + e, NODES, stride=ES), :] for e in (0, 1)], 0)
                for h in (0, 1)
            )
            rows = slice(2 * p * NODES, (2 * p + 2) * NODES)
            ref[rows, :128] = low
            ref[rows, 128:] = high
            ends = pltpu.roll(jnp.where(lane < NODES, low, high), slot + wide, 1)
            tile = jnp.where((lane >= slot) & (lane < slot + 2 * wide), ends, tile)
    for copy in copies[4:]:
        copy.wait()
    columns[...] = tile.T[:32]
    columns[24:25] = own[...].astype(f32)
    columns[25:26] = disp[...]
    span, _ = position()
    for out, top in ((edge_a, span % 2 == 0), (edge_b, span % 2 == 1)):

        @pl.when(top)
        def _():
            out[: 2 * NODES] = src[(ES - 2) * NODES :, :]
            out[2 * NODES :] = cf[(ES - 1) * NODES :, :]

        @pl.when(jnp.logical_not(top))
        def _():
            out[: 2 * NODES] = src[: 2 * NODES, :]
            out[2 * NODES :] = cf[:NODES, :]


def sides(index, first, second):
    even = index % 2 == 0
    return jnp.where(even, second, first), jnp.where(even, first, second)


def pack_corner(cross_a, cross_b, own, disp, first, second):
    span, cross = position()
    half = lax.broadcasted_iota(jnp.int32, (1, 128), 1) < NODES
    left, right = sides(cross, cross_a[...], cross_b[...])
    after = jnp.where(half, pltpu.roll(left[13:14], NODES, 1), right[14:15])
    before = jnp.where(half, left[1:2], pltpu.roll(right[2:3], NODES, 1))
    rows = [left[24:25], own[...].astype(f32), right[24:25], left[25:26], disp[...], right[25:26]]
    rows = jnp.concatenate(rows + [jnp.zeros((1, 128), f32)], 0)
    for out, top in ((first, span % 2 == 0), (second, span % 2 == 1)):
        out[0:1] = jnp.where(top, after, before)
        out[1:8] = rows


def join(cross_a, cross_b, d, out):
    dl, dr = sides(position()[1], cross_a[...], cross_b[...])
    out[...] = jnp.concatenate([dl, d[...], dr], 0)


def product(mats, x, lo, hi):
    xh, xl = parts(x)
    return jnp.dot(
        mats[lo * NODES : hi * NODES, :], jnp.concatenate([xh, xh, xl], 0), preferred_element_type=f32
    )


def spread(sel, cols):
    return lax.dot_general(
        jnp.concatenate(sel, 1), jnp.concatenate(cols, 1), NT, preferred_element_type=f32
    )


def weighted(x, size, value):
    return parts(jnp.where(onehot(x, size), value, 0.0))


def main_part(spot, shift, size, d):
    n, s, x = spot
    sel = pick(onehot((s + shift) * NODES + n, size))
    return spread([sel, sel], weighted(x, EX, d))


def side_part(before, after, shift, size, d_before, d_after):
    (nb, sb, xb), (na, sa, xa) = before, after
    sel_b = pick(onehot((sb + shift) * NODES + nb, size))
    sel_a = pick(onehot((sa + shift) * NODES + na, size))
    cols_b = weighted(jnp.where(xb >= EX - 2, xb - 128, -1), 128, d_before)
    cols_a = weighted(jnp.where(xa < 2, xa, -1), 128, d_after)
    return spread([sel_b, sel_b, sel_a, sel_a], cols_b + cols_a)


def trace(field, spot):
    n, s, x = spot
    cols = pick(onehot(x, EX))
    found = jnp.dot(
        jnp.concatenate(parts(field), 1), jnp.concatenate([cols, cols], 0), preferred_element_type=f32
    )
    return jnp.sum(jnp.where(onehot(s * NODES + n, ES * NODES), found, 0.0), axis=0, keepdims=True)


def inner_kernel(first, *refs):
    if first:
        src, cf, own, disp, *raw, r_out, v_out, tr_out, mats = refs
        for k, ref in enumerate(raw):
            m = ref[...] if k == 0 else -ref[...]
            high = m.astype(bf16).astype(f32)
            mats[at(k), :] = jnp.concatenate([high, m - high, high], 1).astype(bf16)
    else:
        src, cf, own, disp, mats, r_out, v_out, tr_out = refs
    spot = place(own[...])
    r_out[...] = src[...] + main_part(spot, 0, ES * NODES, disp[...])
    lane = lax.broadcasted_iota(jnp.int32, (1, EX), 1)
    low, pending = None, None
    for s in range(ES):
        prod = product(mats, r_out[at(s), :], 0, 5)
        up = prod[2 * NODES : 3 * NODES]
        if s:
            v_out[at(s), :EX] = pending + up
        else:
            v_out[at(0), :EX] = up
        before = pltpu.roll(prod[3 * NODES : 4 * NODES], 1, 1)
        after = pltpu.roll(prod[4 * NODES :], EX - 1, 1)
        pending = (
            cf[at(s), :] * r_out[at(s), :] + prod[:NODES]
            + jnp.where(lane == 0, 0.0, before) + jnp.where(lane == EX - 1, 0.0, after)
        )
        if s:
            pending = pending + low
        v_out[at(s + 1), EX:] = jnp.where(lane[:, :128] == 0, before[:, :128], 0.0) + jnp.where(
            lane[:, :128] == 127, after[:, 128:], 0.0
        )
        low = prod[NODES : 2 * NODES]
    v_out[at(ES), :EX] = pending
    v_out[at(ES + 1), :EX] = low
    tr_out[...] = trace(r_out[...], spot)


def lines(prod, k):
    return prod[k * NODES : (k + 1) * NODES]


def cast(before, after):
    lane = lax.broadcasted_iota(jnp.int32, (1, 128), 1)
    first_lane = jnp.where(lane == 0, pltpu.roll(before, 1, 1), 0.0)
    last_lane = jnp.where(lane == 127, pltpu.roll(after, 127, 1), 0.0)
    return jnp.concatenate([first_lane, last_lane], 1)


def kept_lanes(cross, n_xs):
    lane = lax.broadcasted_iota(jnp.int32, (1, 128), 1)
    return jnp.where((lane == 0) & (cross < n_xs - 1) | (lane == 127) & (cross > 0), 1.0, 0.0).astype(f32)


def side_kernel(first, n_xs, *refs):
    _, cross = position()
    part, mats, cross_a, cross_b, *refs = refs
    left, right = sides(cross, cross_a[...], cross_b[...])
    if first:
        out, wing, edge, w_scr = refs
        d_left, d_right = left[25:26], right[25:26]
        for p in range(4):
            k, rows = 4 * p, slice(2 * p * NODES, (2 * p + 2) * NODES)
            wing[rows, :] = lane_rows(
                ((0, right[k + 2 : k + 3]), (1, right[k + 3 : k + 4]), (126, left[k : k + 1]), (127, left[k + 1 : k + 2]))
            )
            k = 16 + 2 * p
            edge[rows, :] = lane_rows(((0, right[k + 1 : k + 2]), (127, left[k : k + 1])))
    else:
        d_ca, d_cb, wing, edge, out, w_scr = refs
        d_left, d_right = sides(cross, d_ca[...], d_cb[...])
    w_scr[...] = wing[...] + side_part(
        place(left[24:25]), place(right[24:25]), 0, ES * NODES, d_left, d_right
    )
    lane = lax.broadcasted_iota(jnp.int32, (1, 128), 1)
    keep = kept_lanes(cross, n_xs)
    out[at(0), :EX] = part[at(0), :EX]
    out[at(9), :EX] = part[at(9), :EX]

    def pair(s):
        both = product(mats, jnp.concatenate([w_scr[at(s), :], w_scr[at(s + 1), :]], 1), 0, 5)
        return both[:, :128], both[:, 128:]

    old, now = None, pair(0)
    for s in range(0, ES, 2):
        new = pair(s + 2) if s + 2 < ES else None
        for k, prod, down, up in (
            (s, now[0], old and old[1], now[1]), (s + 1, now[1], now[0], new and new[0]),
        ):
            out[at(k + 1), :EX] = part[at(k + 1), :EX] + cast(lines(prod, 3), lines(prod, 4))
            outer = (
                edge[at(k), :] * w_scr[at(k), :] + lines(prod, 0)
                + jnp.where(lane == 0, 0.0, pltpu.roll(lines(prod, 3), 1, 1))
                + jnp.where(lane == 127, 0.0, pltpu.roll(lines(prod, 4), 127, 1))
            )
            if down is not None:
                outer = outer + lines(down, 1)
            if up is not None:
                outer = outer + lines(up, 2)
            out[at(k + 1), EX:] = (part[at(k + 1), EX:] + outer) * keep
        old, now = now, new


def outer_kernel(first, n_xs, *refs):
    span, cross = position()
    cf, r_own, part, tr, mats, small_a, small_b, own, *refs = refs
    i_bel, i_abv = sides(span, small_a[...], small_b[...])
    if first:
        edge_a, edge_b, msg, rim, wing, h_scr, v_scr = refs
        d_bel, d_abv = i_bel[4:7], i_abv[4:7]
        rim[: 3 * NODES], rim[3 * NODES :] = sides(span, edge_a[...], edge_b[...])
        half = lax.broadcasted_iota(jnp.int32, (1, 128), 1) < NODES
        cb, ct = i_bel[0:1], i_abv[0:1]
        wing[...] = lane_rows(
            (
                (0, jnp.where(half, pltpu.roll(cb, NODES, 1), ct)),
                (127, jnp.where(half, cb, pltpu.roll(ct, NODES, 1))),
            )
        )
    else:
        d_a, d_b, rim, wing, msg, v_out, h_scr, v_scr = refs
        d_bel, d_abv = sides(span, d_a[...], d_b[...])
    spot = place(own[...])
    corners = []
    for idx, d, shift, base, turn in ((i_bel, d_bel, 2 - ES, 0, 1 - ES), (i_abv, d_abv, 0, 3 * NODES, 0)):
        spots = [place(idx[k : k + 1]) for k in (1, 2, 3)]
        h_scr[slice(base, base + 2 * NODES), :] = rim[base : base + 2 * NODES] + main_part(
            spots[1], shift, 2 * NODES, d[1:2]
        )
        corners.append(side_part(spots[0], spots[2], turn, NODES, d[0:1], d[2:3]))
    far_b = product(mats, h_scr[at(0), :], 1, 2)
    near_b = product(mats, h_scr[at(1), :], 0, 5)
    near_a = product(mats, h_scr[at(3), :], 0, 5)
    far_a = product(mats, h_scr[at(4), :], 2, 3)
    ends = product(
        mats, jnp.concatenate([wing[at(0), :] + corners[0], wing[at(1), :] + corners[1]], 1), 1, 5
    )
    lane = lax.broadcasted_iota(jnp.int32, (1, 128), 1)
    wide = lax.broadcasted_iota(jnp.int32, (1, EX), 1)
    keep = kept_lanes(cross, n_xs)

    def shifted(prod):
        return jnp.where(wide == 0, 0.0, pltpu.roll(lines(prod, 3), 1, 1)) + jnp.where(
            wide == EX - 1, 0.0, pltpu.roll(lines(prod, 4), EX - 1, 1)
        )

    for s, k, prod, far, lanes in (
        (1, 1, near_b, far_b, slice(0, 128)), (10, 3, near_a, far_a, slice(128, 256)),
    ):
        coef = rim[2 * NODES : 3 * NODES] if s == 1 else rim[5 * NODES :]
        v_scr[at(s, 1), :EX] = (
            part[at(s, 1), :EX] + coef * h_scr[at(k), :] + lines(prod, 0) + far + shifted(prod)
            + cast(ends[2 * NODES : 3 * NODES, lanes], ends[3 * NODES :, lanes])
        )
    v_scr[at(2, 1), :EX] = part[at(2, 1), :EX] + lines(near_b, 1)
    v_scr[at(2, 1), EX:] = part[at(2, 1), EX:] + lines(ends, 0)[:, :128] * keep
    v_scr[at(9, 1), :EX] = part[at(9, 1), :EX] + lines(near_a, 2)
    v_scr[at(9, 1), EX:] = part[at(9, 1), EX:] + lines(ends, 1)[:, 128:] * keep
    v_scr[at(3, 1).start : at(8, 1).stop, :] = part[at(3, 1).start : at(8, 1).stop, :]

    casts = {}
    for s in range(2, 10, 2):
        pair = product(mats, jnp.concatenate([v_scr[at(s, 1), EX:], v_scr[at(s + 1, 1), EX:]], 1), 3, 5)
        casts[s] = cast(pair[:NODES, :128], pair[NODES:, :128])
        casts[s + 1] = cast(pair[:NODES, 128:], pair[NODES:, 128:])
    sums = [jnp.zeros((8, EX), f32) for _ in range(5)]
    low = product(mats, v_scr[at(1, 1), :EX], 1, 2)
    pending = None
    for s in range(2, 11):
        if s < 10:
            prod = product(mats, v_scr[at(s, 1), :EX], 0, 5)
            up = lines(prod, 2)
        else:
            up = product(mats, v_scr[at(s, 1), :EX], 2, 3)
        if pending is not None:
            r, v = r_own[at(s - 1, 2), :], v_scr[at(s - 1, 1), :EX]
            w = pending + up - THETA * v
            pairs = ((v, v), (v, w), (w, w), (r, v), (r, w))
            for k, (a, b) in enumerate(pairs):
                sums[k] = sums[k] + jnp.sum((a * b).reshape(8, 8, EX), axis=0)
        if s < 10:
            pending = (
                cf[at(s, 2), :] * v_scr[at(s, 1), :EX] + lines(prod, 0) + low + casts[s] + shifted(prod)
            )
            low = lines(prod, 1)

    gram = jnp.zeros((1, 128), f32)
    for k in range(5):
        total = jnp.sum(jnp.sum(sums[k], axis=0, keepdims=True), axis=1, keepdims=True)
        gram = gram + jnp.where(lane == k, total, 0.0)
    v_mid = v_scr[NODES : 9 * NODES, :EX]
    rows = [gram, tr[...], trace(v_mid, spot)]
    msg[...] = jnp.broadcast_to(jnp.concatenate(rows, 1)[None], msg.shape)
    if not first:
        v_out[...] = v_mid


def solve(got):
    total = jnp.sum(got[:, 0, :128], axis=0, keepdims=True)
    lane = lax.broadcasted_iota(jnp.int32, (1, 128), 1)
    g11, g12, g22, g1, g2 = (
        jnp.sum(jnp.where(lane == k, total, 0.0), axis=1, keepdims=True) for k in range(5)
    )
    ratio = g12 / g11
    b = (g2 - ratio * g1) / (g22 - ratio * g12)
    a = (g1 - b * g12) / g11
    return a - THETA * b, b


def displace(a, b, got, compliance, disp, out):
    start = position()[0] * 16
    traces = a * got[pl.ds(start, 16), 0, 128:256] + b * got[pl.ds(start, 16), 0, 256:]
    acc = jnp.zeros((IFN, 128), f32)
    for j in range(16):
        acc = acc + compliance[:, j * 128 : (j + 1) * 128] * traces[j : j + 1]
    fresh = jnp.sum(acc.T, axis=0, keepdims=True)
    out[...] = 0.5 * fresh + 0.5 * disp[...]


def shell_kernel(got, compliance, disp, out):
    displace(*solve(got), got, compliance, disp, out)


def final_kernel(got, compliance, disp, r, v, fluid, out):
    a, b = solve(got)
    displace(a, b, got, compliance, disp, out)
    for s in range(ES):
        fluid[:, s, :] = a * r[at(s), :] + b * v[at(s), :]


def call(kernel, outs, ins, scratch=()):
    vm = pl.BlockSpec(memory_space=pltpu.VMEM)
    return pl.pallas_call(
        kernel,
        out_shape=[pltpu.VMEM(*o) for o in outs],
        in_specs=[vm] * len(ins),
        out_specs=[vm] * len(outs),
        scratch_shapes=[pltpu.VMEM(x, f32) for x in scratch],
        compiler_params=pltpu.CompilerParams(vmem_limit_bytes=16 << 20),
    )(*(pltpu.with_memory_space_constraint(x, pltpu.VMEM) for x in ins))


def swaps(axis, wrap):
    size = lax.axis_size(axis)
    pairs = [(i, i + 1) for i in range(size - 1)] + ([(size - 1, 0)] if wrap else [])
    return [[p for i, j in pairs[k::2] for p in ((i, j), (j, i))] for k in (0, 1)]


def body(
    source, coefficient, volume_matrix, span_lower, span_upper, cross_lower,
    cross_upper, interface, compliance, start_displacement,
):
    n_xs = lax.axis_size("xs")
    own, disp, rows = interface[0], start_displacement[0], compliance[0]
    mats = [volume_matrix, span_lower, span_upper, cross_lower, cross_upper]
    message, block = ((128, 1, 3 * 128), f32), ((ES * NODES, EX), f32)
    row, wide = ((1, 128), f32), ((10 * NODES, LANES), f32)

    def trade(axis, a, b):
        first, second = swaps(axis, axis == "span")
        far = lax.ppermute(b, axis, second)
        near = lax.ppermute(a, axis, first)
        return [near, far]

    args = [x.reshape(ES * NODES, EX) for x in (source, coefficient)] + [own, disp] + mats
    far = pl.BlockSpec(memory_space=pl.ANY)
    packed, near_s, far_s, src, cf, own, disp, *mats = pl.pallas_call(
        pack,
        out_shape=[pltpu.VMEM((32, 128), f32)]
        + [pltpu.VMEM((3 * NODES, EX), f32)] * 2
        + [pltpu.VMEM(*block)] * 2
        + [pltpu.VMEM(x.shape, x.dtype) for x in args[2:]],
        in_specs=[far] * 9,
        out_specs=[pl.BlockSpec(memory_space=pltpu.VMEM)] * 12,
        scratch_shapes=[
            pltpu.VMEM((4, ES * NODES, 128), f32), pltpu.SemaphoreType.DMA((11,))
        ],
        compiler_params=pltpu.CompilerParams(vmem_limit_bytes=16 << 20),
        name="pack",
    )(*(pltpu.with_memory_space_constraint(x, pltpu.HBM) for x in args))
    ends = trade("span", near_s, far_s)
    cols = trade("xs", packed, packed)
    r, part, tr, split = call(
        lambda *refs: inner_kernel(True, *refs),
        [block, wide, row, ((5 * NODES, 3 * NODES), bf16)],
        [src, cf, own, disp, *mats],
    )
    small = call(pack_corner, [((8, 128), f32)] * 2, [*cols, own, disp])
    around = [*trade("span", *small), own]
    outers = ((ES * NODES, 128), f32)
    scratch = [(5 * NODES, EX), wide[0]]
    part, *cross = call(
        lambda *refs: side_kernel(True, n_xs, *refs), [wide, outers, outers],
        [part, split, *cols], [outers[0]],
    )
    sent, *static = call(
        lambda *refs: outer_kernel(True, n_xs, *refs),
        [message, ((6 * NODES, EX), f32), ((2 * NODES, 128), f32)],
        [cf, r, part, tr, split, *around, *ends], scratch,
    )
    got = lax.all_to_all(sent, AXES, 0, 0, tiled=True)
    (disp,) = call(shell_kernel, [row], [got, rows, disp])
    beside = trade("xs", disp, disp)
    r, part, tr = call(
        lambda *refs: inner_kernel(False, *refs),
        [block, wide, row], [src, cf, own, disp, split],
    )
    (mid,) = call(join, [((3, 128), f32)], [*beside, disp])
    over = trade("span", mid, mid)
    (part,) = call(
        lambda *refs: side_kernel(False, n_xs, *refs), [wide],
        [part, split, *cols, *beside, *cross], [outers[0]],
    )
    sent, v = call(
        lambda *refs: outer_kernel(False, n_xs, *refs), [message, block],
        [cf, r, part, tr, split, *around, *over, *static], scratch,
    )
    got = lax.all_to_all(sent, AXES, 0, 0, tiled=True)
    near = pl.BlockSpec(memory_space=pltpu.VMEM)
    fluid, disp = pl.pallas_call(
        final_kernel,
        out_shape=[jax.ShapeDtypeStruct((NODES, ES, EX), f32), jax.ShapeDtypeStruct(*row)],
        in_specs=[near] * 5,
        out_specs=[near] * 2,
        compiler_params=pltpu.CompilerParams(vmem_limit_bytes=16 << 20),
        name="final",
    )(*(pltpu.with_memory_space_constraint(x, pltpu.VMEM) for x in (got, rows, disp, r, v)))
    return fluid, disp[None]


def solution(mesh):
    field = P(None, "span", "xs")
    section = P("span", "xs", None)
    return jax.shard_map(
        body,
        mesh=mesh,
        in_specs=(field, field, P(), P(), P(), P(), P(), section, section, section),
        out_specs=(field, section),
        check_vma=False,
    )
```

```python
import jax
import jax.numpy as jnp
from jax import lax
from jax.experimental import pallas as pl
from jax.experimental.pallas import tpu as pltpu
from jax.sharding import PartitionSpec as P


NODES, ES, EX, IFN = 64, 8, 256, 128
LANES = EX + 128
AXES = ("span", "xs")
THETA = 3.75
f32 = jnp.float32
bf16 = jnp.bfloat16
NT = (((1,), (1,)), ((), ()))


def parts(x):
    hi = x.astype(bf16)
    return hi, (x - hi.astype(f32)).astype(bf16)


def place(i):
    i = i.astype(jnp.int32)
    return i >> 11, (i >> 8) & 7, i & 255


def onehot(pos, size):
    rows = lax.broadcasted_iota(jnp.int32, (size, IFN), 0)
    return rows == pos


def pick(mask):
    return jnp.where(mask, 1.0, 0.0).astype(bf16)


def lane_rows(entries):
    rows = lax.broadcasted_iota(jnp.int32, (128, 128), 0)
    tile = jnp.zeros((128, 128), f32)
    for pos, value in entries:
        tile = jnp.where(rows == pos, value, tile)
    return tile.T


def at(s, first=0):
    return slice((s - first) * NODES, (s - first + 1) * NODES)


def position():
    return lax.axis_index("span"), lax.axis_index("xs")


def pack(*refs):
    far, (columns, edge_a, edge_b, *near, halves, sems) = refs[:9], refs[9:]
    src, cf, own, disp, *_ = near
    pairs = [(f.at[:, pl.ds(h * 128, 128)], halves.at[2 * k + h]) for k, f in enumerate(far[:2]) for h in (0, 1)]
    pairs += list(zip(far[2:], near[2:]))
    copies = [pltpu.make_async_copy(a, b, sems.at[k]) for k, (a, b) in enumerate(pairs)]
    for copy in copies:
        copy.start()
    lane = lax.broadcasted_iota(jnp.int32, (1, 128), 1)
    tile = jnp.zeros((2 * NODES, 128), f32)
    for k, (ref, wide, base) in enumerate(((src, 2, 0), (cf, 1, 16))):
        copies[2 * k].wait()
        copies[2 * k + 1].wait()
        for p in range(4):
            slot = base + 2 * wide * p
            low, high = (
                jnp.concatenate([halves[2 * k + h, pl.ds(2 * p + e, NODES, stride=ES), :] for e in (0, 1)], 0)
                for h in (0, 1)
            )
            rows = slice(2 * p * NODES, (2 * p + 2) * NODES)
            ref[rows, :128] = low
            ref[rows, 128:] = high
            ends = pltpu.roll(jnp.where(lane < NODES, low, high), slot + wide, 1)
            tile = jnp.where((lane >= slot) & (lane < slot + 2 * wide), ends, tile)
    for copy in copies[4:]:
        copy.wait()
    columns[...] = tile.T[:32]
    columns[24:25] = own[...].astype(f32)
    columns[25:26] = disp[...]
    span, _ = position()
    for out, top in ((edge_a, span % 2 == 0), (edge_b, span % 2 == 1)):

        @pl.when(top)
        def _():
            out[: 2 * NODES] = src[(ES - 2) * NODES :, :]
            out[2 * NODES :] = cf[(ES - 1) * NODES :, :]

        @pl.when(jnp.logical_not(top))
        def _():
            out[: 2 * NODES] = src[: 2 * NODES, :]
            out[2 * NODES :] = cf[:NODES, :]


def sides(index, first, second):
    even = index % 2 == 0
    return jnp.where(even, second, first), jnp.where(even, first, second)


def pack_corner(cross_a, cross_b, own, disp, first, second):
    span, cross = position()
    half = lax.broadcasted_iota(jnp.int32, (1, 128), 1) < NODES
    left, right = sides(cross, cross_a[...], cross_b[...])
    after = jnp.where(half, pltpu.roll(left[13:14], NODES, 1), right[14:15])
    before = jnp.where(half, left[1:2], pltpu.roll(right[2:3], NODES, 1))
    rows = [left[24:25], own[...].astype(f32), right[24:25], left[25:26], disp[...], right[25:26]]
    rows = jnp.concatenate(rows + [jnp.zeros((1, 128), f32)], 0)
    for out, top in ((first, span % 2 == 0), (second, span % 2 == 1)):
        out[0:1] = jnp.where(top, after, before)
        out[1:8] = rows


def join(cross_a, cross_b, d, out):
    dl, dr = sides(position()[1], cross_a[...], cross_b[...])
    out[...] = jnp.concatenate([dl, d[...], dr], 0)


def product(mats, x, lo, hi):
    xh, xl = parts(x)
    return jnp.dot(
        mats[lo * NODES : hi * NODES, :], jnp.concatenate([xh, xh, xl], 0), preferred_element_type=f32
    )


def spread(sel, cols):
    return lax.dot_general(
        jnp.concatenate(sel, 1), jnp.concatenate(cols, 1), NT, preferred_element_type=f32
    )


def weighted(x, size, value):
    return parts(jnp.where(onehot(x, size), value, 0.0))


def main_part(spot, shift, size, d):
    n, s, x = spot
    sel = pick(onehot((s + shift) * NODES + n, size))
    return spread([sel, sel], weighted(x, EX, d))


def side_part(before, after, shift, size, d_before, d_after):
    (nb, sb, xb), (na, sa, xa) = before, after
    sel_b = pick(onehot((sb + shift) * NODES + nb, size))
    sel_a = pick(onehot((sa + shift) * NODES + na, size))
    cols_b = weighted(jnp.where(xb >= EX - 2, xb - 128, -1), 128, d_before)
    cols_a = weighted(jnp.where(xa < 2, xa, -1), 128, d_after)
    return spread([sel_b, sel_b, sel_a, sel_a], cols_b + cols_a)


def trace(field, spot):
    n, s, x = spot
    cols = pick(onehot(x, EX))
    found = jnp.dot(
        jnp.concatenate(parts(field), 1), jnp.concatenate([cols, cols], 0), preferred_element_type=f32
    )
    return jnp.sum(jnp.where(onehot(s * NODES + n, ES * NODES), found, 0.0), axis=0, keepdims=True)


def inner_kernel(first, *refs):
    if first:
        src, cf, own, disp, *raw, r_out, v_out, tr_out, mats = refs
        for k, ref in enumerate(raw):
            m = ref[...] if k == 0 else -ref[...]
            high = m.astype(bf16).astype(f32)
            mats[at(k), :] = jnp.concatenate([high, m - high, high], 1).astype(bf16)
    else:
        src, cf, own, disp, mats, r_out, v_out, tr_out = refs
    spot = place(own[...])
    r_out[...] = src[...] + main_part(spot, 0, ES * NODES, disp[...])
    lane = lax.broadcasted_iota(jnp.int32, (1, EX), 1)
    low, pending = None, None
    for s in range(ES):
        prod = product(mats, r_out[at(s), :], 0, 5)
        up = prod[2 * NODES : 3 * NODES]
        if s:
            v_out[at(s), :EX] = pending + up
        else:
            v_out[at(0), :EX] = up
        before = pltpu.roll(prod[3 * NODES : 4 * NODES], 1, 1)
        after = pltpu.roll(prod[4 * NODES :], EX - 1, 1)
        pending = (
            cf[at(s), :] * r_out[at(s), :] + prod[:NODES]
            + jnp.where(lane == 0, 0.0, before) + jnp.where(lane == EX - 1, 0.0, after)
        )
        if s:
            pending = pending + low
        v_out[at(s + 1), EX:] = jnp.where(lane[:, :128] == 0, before[:, :128], 0.0) + jnp.where(
            lane[:, :128] == 127, after[:, 128:], 0.0
        )
        low = prod[NODES : 2 * NODES]
    v_out[at(ES), :EX] = pending
    v_out[at(ES + 1), :EX] = low
    tr_out[...] = trace(r_out[...], spot)


def lines(prod, k):
    return prod[k * NODES : (k + 1) * NODES]


def cast(before, after):
    lane = lax.broadcasted_iota(jnp.int32, (1, 128), 1)
    first_lane = jnp.where(lane == 0, pltpu.roll(before, 1, 1), 0.0)
    last_lane = jnp.where(lane == 127, pltpu.roll(after, 127, 1), 0.0)
    return jnp.concatenate([first_lane, last_lane], 1)


def kept_lanes(cross, n_xs):
    lane = lax.broadcasted_iota(jnp.int32, (1, 128), 1)
    return jnp.where((lane == 0) & (cross < n_xs - 1) | (lane == 127) & (cross > 0), 1.0, 0.0).astype(f32)


def side_kernel(first, n_xs, *refs):
    _, cross = position()
    part, mats, cross_a, cross_b, *refs = refs
    left, right = sides(cross, cross_a[...], cross_b[...])
    if first:
        out, wing, edge, w_scr = refs
        d_left, d_right = left[25:26], right[25:26]
        for p in range(4):
            k, rows = 4 * p, slice(2 * p * NODES, (2 * p + 2) * NODES)
            wing[rows, :] = lane_rows(
                ((0, right[k + 2 : k + 3]), (1, right[k + 3 : k + 4]), (126, left[k : k + 1]), (127, left[k + 1 : k + 2]))
            )
            k = 16 + 2 * p
            edge[rows, :] = lane_rows(((0, right[k + 1 : k + 2]), (127, left[k : k + 1])))
    else:
        d_ca, d_cb, wing, edge, out, w_scr = refs
        d_left, d_right = sides(cross, d_ca[...], d_cb[...])
    w_scr[...] = wing[...] + side_part(
        place(left[24:25]), place(right[24:25]), 0, ES * NODES, d_left, d_right
    )
    lane = lax.broadcasted_iota(jnp.int32, (1, 128), 1)
    keep = kept_lanes(cross, n_xs)
    out[at(0), :EX] = part[at(0), :EX]
    out[at(9), :EX] = part[at(9), :EX]

    def pair(s):
        both = product(mats, jnp.concatenate([w_scr[at(s), :], w_scr[at(s + 1), :]], 1), 0, 5)
        return both[:, :128], both[:, 128:]

    old, now = None, pair(0)
    for s in range(0, ES, 2):
        new = pair(s + 2) if s + 2 < ES else None
        for k, prod, down, up in (
            (s, now[0], old and old[1], now[1]), (s + 1, now[1], now[0], new and new[0]),
        ):
            out[at(k + 1), :EX] = part[at(k + 1), :EX] + cast(lines(prod, 3), lines(prod, 4))
            outer = (
                edge[at(k), :] * w_scr[at(k), :] + lines(prod, 0)
                + jnp.where(lane == 0, 0.0, pltpu.roll(lines(prod, 3), 1, 1))
                + jnp.where(lane == 127, 0.0, pltpu.roll(lines(prod, 4), 127, 1))
            )
            if down is not None:
                outer = outer + lines(down, 1)
            if up is not None:
                outer = outer + lines(up, 2)
            out[at(k + 1), EX:] = (part[at(k + 1), EX:] + outer) * keep
        old, now = now, new


def outer_kernel(first, n_xs, *refs):
    span, cross = position()
    cf, r_own, part, tr, mats, small_a, small_b, own, *refs = refs
    i_bel, i_abv = sides(span, small_a[...], small_b[...])
    if first:
        edge_a, edge_b, msg, rim, wing, h_scr, v_scr = refs
        d_bel, d_abv = i_bel[4:7], i_abv[4:7]
        rim[: 3 * NODES], rim[3 * NODES :] = sides(span, edge_a[...], edge_b[...])
        half = lax.broadcasted_iota(jnp.int32, (1, 128), 1) < NODES
        cb, ct = i_bel[0:1], i_abv[0:1]
        wing[...] = lane_rows(
            (
                (0, jnp.where(half, pltpu.roll(cb, NODES, 1), ct)),
                (127, jnp.where(half, cb, pltpu.roll(ct, NODES, 1))),
            )
        )
    else:
        d_a, d_b, rim, wing, msg, v_out, h_scr, v_scr = refs
        d_bel, d_abv = sides(span, d_a[...], d_b[...])
    spot = place(own[...])
    corners = []
    for idx, d, shift, base, turn in ((i_bel, d_bel, 2 - ES, 0, 1 - ES), (i_abv, d_abv, 0, 3 * NODES, 0)):
        spots = [place(idx[k : k + 1]) for k in (1, 2, 3)]
        h_scr[slice(base, base + 2 * NODES), :] = rim[base : base + 2 * NODES] + main_part(
            spots[1], shift, 2 * NODES, d[1:2]
        )
        corners.append(side_part(spots[0], spots[2], turn, NODES, d[0:1], d[2:3]))
    far_b = product(mats, h_scr[at(0), :], 1, 2)
    near_b = product(mats, h_scr[at(1), :], 0, 5)
    near_a = product(mats, h_scr[at(3), :], 0, 5)
    far_a = product(mats, h_scr[at(4), :], 2, 3)
    ends = product(
        mats, jnp.concatenate([wing[at(0), :] + corners[0], wing[at(1), :] + corners[1]], 1), 1, 5
    )
    lane = lax.broadcasted_iota(jnp.int32, (1, 128), 1)
    wide = lax.broadcasted_iota(jnp.int32, (1, EX), 1)
    keep = kept_lanes(cross, n_xs)

    def shifted(prod):
        return jnp.where(wide == 0, 0.0, pltpu.roll(lines(prod, 3), 1, 1)) + jnp.where(
            wide == EX - 1, 0.0, pltpu.roll(lines(prod, 4), EX - 1, 1)
        )

    for s, k, prod, far, lanes in (
        (1, 1, near_b, far_b, slice(0, 128)), (10, 3, near_a, far_a, slice(128, 256)),
    ):
        coef = rim[2 * NODES : 3 * NODES] if s == 1 else rim[5 * NODES :]
        v_scr[at(s, 1), :EX] = (
            part[at(s, 1), :EX] + coef * h_scr[at(k), :] + lines(prod, 0) + far + shifted(prod)
            + cast(ends[2 * NODES : 3 * NODES, lanes], ends[3 * NODES :, lanes])
        )
    v_scr[at(2, 1), :EX] = part[at(2, 1), :EX] + lines(near_b, 1)
    v_scr[at(2, 1), EX:] = part[at(2, 1), EX:] + lines(ends, 0)[:, :128] * keep
    v_scr[at(9, 1), :EX] = part[at(9, 1), :EX] + lines(near_a, 2)
    v_scr[at(9, 1), EX:] = part[at(9, 1), EX:] + lines(ends, 1)[:, 128:] * keep
    v_scr[at(3, 1).start : at(8, 1).stop, :] = part[at(3, 1).start : at(8, 1).stop, :]

    casts = {}
    for s in range(2, 10, 2):
        pair = product(mats, jnp.concatenate([v_scr[at(s, 1), EX:], v_scr[at(s + 1, 1), EX:]], 1), 3, 5)
        casts[s] = cast(pair[:NODES, :128], pair[NODES:, :128])
        casts[s + 1] = cast(pair[:NODES, 128:], pair[NODES:, 128:])
    sums = [jnp.zeros((8, EX), f32) for _ in range(5)]
    low = product(mats, v_scr[at(1, 1), :EX], 1, 2)
    pending = None
    for s in range(2, 11):
        if s < 10:
            prod = product(mats, v_scr[at(s, 1), :EX], 0, 5)
            up = lines(prod, 2)
        else:
            up = product(mats, v_scr[at(s, 1), :EX], 2, 3)
        if pending is not None:
            r, v = r_own[at(s - 1, 2), :], v_scr[at(s - 1, 1), :EX]
            w = pending + up - THETA * v
            pairs = ((v, v), (v, w), (w, w), (r, v), (r, w))
            for k, (a, b) in enumerate(pairs):
                sums[k] = sums[k] + jnp.sum((a * b).reshape(8, 8, EX), axis=0)
        if s < 10:
            pending = (
                cf[at(s, 2), :] * v_scr[at(s, 1), :EX] + lines(prod, 0) + low + casts[s] + shifted(prod)
            )
            low = lines(prod, 1)

    gram = jnp.zeros((1, 128), f32)
    for k in range(5):
        total = jnp.sum(jnp.sum(sums[k], axis=0, keepdims=True), axis=1, keepdims=True)
        gram = gram + jnp.where(lane == k, total, 0.0)
    v_mid = v_scr[NODES : 9 * NODES, :EX]
    rows = [gram, tr[...], trace(v_mid, spot)]
    msg[...] = jnp.broadcast_to(jnp.concatenate(rows, 1)[None], msg.shape)
    if not first:
        v_out[...] = v_mid


def solve(got):
    total = jnp.sum(got[:, 0, :128], axis=0, keepdims=True)
    lane = lax.broadcasted_iota(jnp.int32, (1, 128), 1)
    g11, g12, g22, g1, g2 = (
        jnp.sum(jnp.where(lane == k, total, 0.0), axis=1, keepdims=True) for k in range(5)
    )
    ratio = g12 / g11
    b = (g2 - ratio * g1) / (g22 - ratio * g12)
    a = (g1 - b * g12) / g11
    return a - THETA * b, b


def displace(a, b, got, compliance, disp, out):
    start = position()[0] * 16
    traces = a * got[pl.ds(start, 16), 0, 128:256] + b * got[pl.ds(start, 16), 0, 256:]
    acc = jnp.zeros((IFN, 128), f32)
    for j in range(16):
        acc = acc + compliance[:, j * 128 : (j + 1) * 128] * traces[j : j + 1]
    fresh = jnp.sum(acc.T, axis=0, keepdims=True)
    out[...] = 0.5 * fresh + 0.5 * disp[...]


def shell_kernel(got, compliance, disp, out):
    displace(*solve(got), got, compliance, disp, out)


def final_kernel(got, compliance, disp, r, v, fluid, out):
    a, b = solve(got)
    displace(a, b, got, compliance, disp, out)
    for s in range(ES):
        field = a * r[at(s), :] + b * v[at(s), :]
        for h in (0, 1):
            fluid[pl.ds(h * ES + s, NODES, stride=2 * ES), :] = field[:, h * 128 : (h + 1) * 128]


def call(kernel, outs, ins, scratch=()):
    vm = pl.BlockSpec(memory_space=pltpu.VMEM)
    return pl.pallas_call(
        kernel,
        out_shape=[pltpu.VMEM(*o) for o in outs],
        in_specs=[vm] * len(ins),
        out_specs=[vm] * len(outs),
        scratch_shapes=[pltpu.VMEM(x, f32) for x in scratch],
        compiler_params=pltpu.CompilerParams(vmem_limit_bytes=16 << 20),
    )(*(pltpu.with_memory_space_constraint(x, pltpu.VMEM) for x in ins))


def swaps(axis, wrap):
    size = lax.axis_size(axis)
    pairs = [(i, i + 1) for i in range(size - 1)] + ([(size - 1, 0)] if wrap else [])
    return [[p for i, j in pairs[k::2] for p in ((i, j), (j, i))] for k in (0, 1)]


def body(
    source, coefficient, volume_matrix, span_lower, span_upper, cross_lower,
    cross_upper, interface, compliance, start_displacement,
):
    n_xs = lax.axis_size("xs")
    own, disp, rows = interface[0], start_displacement[0], compliance[0]
    mats = [volume_matrix, span_lower, span_upper, cross_lower, cross_upper]
    message, block = ((128, 1, 3 * 128), f32), ((ES * NODES, EX), f32)
    row, wide = ((1, 128), f32), ((10 * NODES, LANES), f32)

    def trade(axis, a, b):
        first, second = swaps(axis, axis == "span")
        far = lax.ppermute(b, axis, second)
        near = lax.ppermute(a, axis, first)
        return [near, far]

    args = [x.reshape(ES * NODES, EX) for x in (source, coefficient)] + [own, disp] + mats
    far = pl.BlockSpec(memory_space=pl.ANY)
    packed, near_s, far_s, src, cf, own, disp, *mats = pl.pallas_call(
        pack,
        out_shape=[pltpu.VMEM((32, 128), f32)]
        + [pltpu.VMEM((3 * NODES, EX), f32)] * 2
        + [pltpu.VMEM(*block)] * 2
        + [pltpu.VMEM(x.shape, x.dtype) for x in args[2:]],
        in_specs=[far] * 9,
        out_specs=[pl.BlockSpec(memory_space=pltpu.VMEM)] * 12,
        scratch_shapes=[
            pltpu.VMEM((4, ES * NODES, 128), f32), pltpu.SemaphoreType.DMA((11,))
        ],
        compiler_params=pltpu.CompilerParams(vmem_limit_bytes=16 << 20),
        name="pack",
    )(*(pltpu.with_memory_space_constraint(x, pltpu.HBM) for x in args))
    ends = trade("span", near_s, far_s)
    cols = trade("xs", packed, packed)
    r, part, tr, split = call(
        lambda *refs: inner_kernel(True, *refs),
        [block, wide, row, ((5 * NODES, 3 * NODES), bf16)],
        [src, cf, own, disp, *mats],
    )
    small = call(pack_corner, [((8, 128), f32)] * 2, [*cols, own, disp])
    around = [*trade("span", *small), own]
    outers = ((ES * NODES, 128), f32)
    scratch = [(5 * NODES, EX), wide[0]]
    part, *cross = call(
        lambda *refs: side_kernel(True, n_xs, *refs), [wide, outers, outers],
        [part, split, *cols], [outers[0]],
    )
    sent, *static = call(
        lambda *refs: outer_kernel(True, n_xs, *refs),
        [message, ((6 * NODES, EX), f32), ((2 * NODES, 128), f32)],
        [cf, r, part, tr, split, *around, *ends], scratch,
    )
    got = lax.all_to_all(sent, AXES, 0, 0, tiled=True)
    (disp,) = call(shell_kernel, [row], [got, rows, disp])
    beside = trade("xs", disp, disp)
    r, part, tr = call(
        lambda *refs: inner_kernel(False, *refs),
        [block, wide, row], [src, cf, own, disp, split],
    )
    (mid,) = call(join, [((3, 128), f32)], [*beside, disp])
    over = trade("span", mid, mid)
    (part,) = call(
        lambda *refs: side_kernel(False, n_xs, *refs), [wide],
        [part, split, *cols, *beside, *cross], [outers[0]],
    )
    sent, v = call(
        lambda *refs: outer_kernel(False, n_xs, *refs), [message, block],
        [cf, r, part, tr, split, *around, *over, *static], scratch,
    )
    got = lax.all_to_all(sent, AXES, 0, 0, tiled=True)
    near = pl.BlockSpec(memory_space=pltpu.VMEM)
    fluid, disp = pl.pallas_call(
        final_kernel,
        out_shape=[jax.ShapeDtypeStruct((2 * ES * NODES, 128), f32), jax.ShapeDtypeStruct(*row)],
        in_specs=[near] * 5,
        out_specs=[near] * 2,
        compiler_params=pltpu.CompilerParams(vmem_limit_bytes=16 << 20),
        name="final",
    )(*(pltpu.with_memory_space_constraint(x, pltpu.VMEM) for x in (got, rows, disp, r, v)))
    fluid = fluid.reshape(NODES, 2, ES, 128).transpose(0, 2, 1, 3)
    return fluid.reshape(source.shape), disp[None]


def solution(mesh):
    field = P(None, "span", "xs")
    section = P("span", "xs", None)
    return jax.shard_map(
        body,
        mesh=mesh,
        in_specs=(field, field, P(), P(), P(), P(), P(), section, section, section),
        out_specs=(field, section),
        check_vma=False,
    )
```

```python
import jax
import jax.numpy as jnp
from jax import lax
from jax.experimental import pallas as pl
from jax.experimental.pallas import tpu as pltpu
from jax.sharding import PartitionSpec as P


NODES, ES, EX, IFN = 64, 8, 256, 128
LANES = EX + 128
AXES = ("span", "xs")
THETA = 3.75
f32 = jnp.float32
bf16 = jnp.bfloat16
NT = (((1,), (1,)), ((), ()))


def parts(x):
    hi = x.astype(bf16)
    return hi, (x - hi.astype(f32)).astype(bf16)


def place(i):
    i = i.astype(jnp.int32)
    return i >> 11, (i >> 8) & 7, i & 255


def onehot(pos, size):
    rows = lax.broadcasted_iota(jnp.int32, (size, IFN), 0)
    return rows == pos


def pick(mask):
    return jnp.where(mask, 1.0, 0.0).astype(bf16)


def lane_rows(entries):
    rows = lax.broadcasted_iota(jnp.int32, (128, 128), 0)
    tile = jnp.zeros((128, 128), f32)
    for pos, value in entries:
        tile = jnp.where(rows == pos, value, tile)
    return tile.T


def at(s, first=0):
    return slice((s - first) * NODES, (s - first + 1) * NODES)


def position():
    return lax.axis_index("span"), lax.axis_index("xs")


def pack(*refs):
    far, (columns, edge_a, edge_b, *near, halves, sems) = refs[:9], refs[9:]
    src, cf, own, disp, *_ = near
    pairs = [(f.at[:, pl.ds(h * 128, 128)], halves.at[2 * k + h]) for k, f in enumerate(far[:2]) for h in (0, 1)]
    pairs += list(zip(far[2:], near[2:]))
    copies = [pltpu.make_async_copy(a, b, sems.at[k]) for k, (a, b) in enumerate(pairs)]
    for copy in copies:
        copy.start()
    lane = lax.broadcasted_iota(jnp.int32, (1, 128), 1)
    tile = jnp.zeros((2 * NODES, 128), f32)
    for k, (ref, wide, base) in enumerate(((src, 2, 0), (cf, 1, 16))):
        copies[2 * k].wait()
        copies[2 * k + 1].wait()
        for p in range(4):
            slot = base + 2 * wide * p
            low, high = (
                jnp.concatenate([halves[2 * k + h, pl.ds(2 * p + e, NODES, stride=ES), :] for e in (0, 1)], 0)
                for h in (0, 1)
            )
            rows = slice(2 * p * NODES, (2 * p + 2) * NODES)
            ref[rows, :128] = low
            ref[rows, 128:] = high
            ends = pltpu.roll(jnp.where(lane < NODES, low, high), slot + wide, 1)
            tile = jnp.where((lane >= slot) & (lane < slot + 2 * wide), ends, tile)
    for copy in copies[4:]:
        copy.wait()
    columns[...] = tile.T[:32]
    columns[24:25] = own[...].astype(f32)
    columns[25:26] = disp[...]
    span, _ = position()
    for out, top in ((edge_a, span % 2 == 0), (edge_b, span % 2 == 1)):

        @pl.when(top)
        def _():
            out[: 2 * NODES] = src[(ES - 2) * NODES :, :]
            out[2 * NODES :] = cf[(ES - 1) * NODES :, :]

        @pl.when(jnp.logical_not(top))
        def _():
            out[: 2 * NODES] = src[: 2 * NODES, :]
            out[2 * NODES :] = cf[:NODES, :]


def sides(index, first, second):
    even = index % 2 == 0
    return jnp.where(even, second, first), jnp.where(even, first, second)


def pack_corner(cross_a, cross_b, own, disp, first, second):
    span, cross = position()
    half = lax.broadcasted_iota(jnp.int32, (1, 128), 1) < NODES
    left, right = sides(cross, cross_a[...], cross_b[...])
    after = jnp.where(half, pltpu.roll(left[13:14], NODES, 1), right[14:15])
    before = jnp.where(half, left[1:2], pltpu.roll(right[2:3], NODES, 1))
    rows = [left[24:25], own[...].astype(f32), right[24:25], left[25:26], disp[...], right[25:26]]
    rows = jnp.concatenate(rows + [jnp.zeros((1, 128), f32)], 0)
    for out, top in ((first, span % 2 == 0), (second, span % 2 == 1)):
        out[0:1] = jnp.where(top, after, before)
        out[1:8] = rows


def join(cross_a, cross_b, d, out):
    dl, dr = sides(position()[1], cross_a[...], cross_b[...])
    out[...] = jnp.concatenate([dl, d[...], dr], 0)


def product(mats, x, lo, hi):
    xh, xl = parts(x)
    return jnp.dot(
        mats[lo * NODES : hi * NODES, :], jnp.concatenate([xh, xh, xl], 0), preferred_element_type=f32
    )


def spread(sel, cols):
    return lax.dot_general(
        jnp.concatenate(sel, 1), jnp.concatenate(cols, 1), NT, preferred_element_type=f32
    )


def weighted(x, size, value):
    return parts(jnp.where(onehot(x, size), value, 0.0))


def main_part(spot, shift, size, d):
    n, s, x = spot
    sel = pick(onehot((s + shift) * NODES + n, size))
    return spread([sel, sel], weighted(x, EX, d))


def side_part(before, after, shift, size, d_before, d_after):
    (nb, sb, xb), (na, sa, xa) = before, after
    sel_b = pick(onehot((sb + shift) * NODES + nb, size))
    sel_a = pick(onehot((sa + shift) * NODES + na, size))
    cols_b = weighted(jnp.where(xb >= EX - 2, xb - 128, -1), 128, d_before)
    cols_a = weighted(jnp.where(xa < 2, xa, -1), 128, d_after)
    return spread([sel_b, sel_b, sel_a, sel_a], cols_b + cols_a)


def trace(field, spot):
    n, s, x = spot
    cols = pick(onehot(x, EX))
    found = jnp.dot(
        jnp.concatenate(parts(field), 1), jnp.concatenate([cols, cols], 0), preferred_element_type=f32
    )
    return jnp.sum(jnp.where(onehot(s * NODES + n, ES * NODES), found, 0.0), axis=0, keepdims=True)


def inner_kernel(first, *refs):
    if first:
        src, cf, own, disp, *raw, r_out, v_out, tr_out, mats = refs
        for k, ref in enumerate(raw):
            m = ref[...] if k == 0 else -ref[...]
            high = m.astype(bf16).astype(f32)
            mats[at(k), :] = jnp.concatenate([high, m - high, high], 1).astype(bf16)
    else:
        src, cf, own, disp, mats, r_out, v_out, tr_out = refs
    spot = place(own[...])
    r_out[...] = src[...] + main_part(spot, 0, ES * NODES, disp[...])
    lane = lax.broadcasted_iota(jnp.int32, (1, EX), 1)
    low, pending = None, None
    for s in range(ES):
        prod = product(mats, r_out[at(s), :], 0, 5)
        up = prod[2 * NODES : 3 * NODES]
        if s:
            v_out[at(s), :EX] = pending + up
        else:
            v_out[at(0), :EX] = up
        before = pltpu.roll(prod[3 * NODES : 4 * NODES], 1, 1)
        after = pltpu.roll(prod[4 * NODES :], EX - 1, 1)
        pending = (
            cf[at(s), :] * r_out[at(s), :] + prod[:NODES]
            + jnp.where(lane == 0, 0.0, before) + jnp.where(lane == EX - 1, 0.0, after)
        )
        if s:
            pending = pending + low
        v_out[at(s + 1), EX:] = jnp.where(lane[:, :128] == 0, before[:, :128], 0.0) + jnp.where(
            lane[:, :128] == 127, after[:, 128:], 0.0
        )
        low = prod[NODES : 2 * NODES]
    v_out[at(ES), :EX] = pending
    v_out[at(ES + 1), :EX] = low
    tr_out[...] = trace(r_out[...], spot)


def lines(prod, k):
    return prod[k * NODES : (k + 1) * NODES]


def cast(before, after):
    lane = lax.broadcasted_iota(jnp.int32, (1, 128), 1)
    first_lane = jnp.where(lane == 0, pltpu.roll(before, 1, 1), 0.0)
    last_lane = jnp.where(lane == 127, pltpu.roll(after, 127, 1), 0.0)
    return jnp.concatenate([first_lane, last_lane], 1)


def kept_lanes(cross, n_xs):
    lane = lax.broadcasted_iota(jnp.int32, (1, 128), 1)
    return jnp.where((lane == 0) & (cross < n_xs - 1) | (lane == 127) & (cross > 0), 1.0, 0.0).astype(f32)


def side_kernel(first, n_xs, *refs):
    _, cross = position()
    part, mats, cross_a, cross_b, *refs = refs
    left, right = sides(cross, cross_a[...], cross_b[...])
    if first:
        out, wing, edge, w_scr = refs
        d_left, d_right = left[25:26], right[25:26]
        for p in range(4):
            k, rows = 4 * p, slice(2 * p * NODES, (2 * p + 2) * NODES)
            wing[rows, :] = lane_rows(
                ((0, right[k + 2 : k + 3]), (1, right[k + 3 : k + 4]), (126, left[k : k + 1]), (127, left[k + 1 : k + 2]))
            )
            k = 16 + 2 * p
            edge[rows, :] = lane_rows(((0, right[k + 1 : k + 2]), (127, left[k : k + 1])))
    else:
        d_ca, d_cb, wing, edge, out, w_scr = refs
        d_left, d_right = sides(cross, d_ca[...], d_cb[...])
    w_scr[...] = wing[...] + side_part(
        place(left[24:25]), place(right[24:25]), 0, ES * NODES, d_left, d_right
    )
    lane = lax.broadcasted_iota(jnp.int32, (1, 128), 1)
    keep = kept_lanes(cross, n_xs)
    out[at(0), :EX] = part[at(0), :EX]
    out[at(9), :EX] = part[at(9), :EX]

    def pair(s):
        both = product(mats, jnp.concatenate([w_scr[at(s), :], w_scr[at(s + 1), :]], 1), 0, 5)
        return both[:, :128], both[:, 128:]

    old, now = None, pair(0)
    for s in range(0, ES, 2):
        new = pair(s + 2) if s + 2 < ES else None
        for k, prod, down, up in (
            (s, now[0], old and old[1], now[1]), (s + 1, now[1], now[0], new and new[0]),
        ):
            out[at(k + 1), :EX] = part[at(k + 1), :EX] + cast(lines(prod, 3), lines(prod, 4))
            outer = (
                edge[at(k), :] * w_scr[at(k), :] + lines(prod, 0)
                + jnp.where(lane == 0, 0.0, pltpu.roll(lines(prod, 3), 1, 1))
                + jnp.where(lane == 127, 0.0, pltpu.roll(lines(prod, 4), 127, 1))
            )
            if down is not None:
                outer = outer + lines(down, 1)
            if up is not None:
                outer = outer + lines(up, 2)
            out[at(k + 1), EX:] = (part[at(k + 1), EX:] + outer) * keep
        old, now = now, new


def outer_kernel(first, n_xs, *refs):
    span, cross = position()
    cf, r_own, part, tr, mats, small_a, small_b, own, *refs = refs
    i_bel, i_abv = sides(span, small_a[...], small_b[...])
    if first:
        edge_a, edge_b, msg, rim, wing, h_scr, v_scr = refs
        d_bel, d_abv = i_bel[4:7], i_abv[4:7]
        rim[: 3 * NODES], rim[3 * NODES :] = sides(span, edge_a[...], edge_b[...])
        half = lax.broadcasted_iota(jnp.int32, (1, 128), 1) < NODES
        cb, ct = i_bel[0:1], i_abv[0:1]
        wing[...] = lane_rows(
            (
                (0, jnp.where(half, pltpu.roll(cb, NODES, 1), ct)),
                (127, jnp.where(half, cb, pltpu.roll(ct, NODES, 1))),
            )
        )
    else:
        d_a, d_b, rim, wing, msg, v_out, h_scr, v_scr = refs
        d_bel, d_abv = sides(span, d_a[...], d_b[...])
    spot = place(own[...])
    corners = []
    for idx, d, shift, base, turn in ((i_bel, d_bel, 2 - ES, 0, 1 - ES), (i_abv, d_abv, 0, 3 * NODES, 0)):
        spots = [place(idx[k : k + 1]) for k in (1, 2, 3)]
        h_scr[slice(base, base + 2 * NODES), :] = rim[base : base + 2 * NODES] + main_part(
            spots[1], shift, 2 * NODES, d[1:2]
        )
        corners.append(side_part(spots[0], spots[2], turn, NODES, d[0:1], d[2:3]))
    far_b = product(mats, h_scr[at(0), :], 1, 2)
    near_b = product(mats, h_scr[at(1), :], 0, 5)
    near_a = product(mats, h_scr[at(3), :], 0, 5)
    far_a = product(mats, h_scr[at(4), :], 2, 3)
    ends = product(
        mats, jnp.concatenate([wing[at(0), :] + corners[0], wing[at(1), :] + corners[1]], 1), 1, 5
    )
    lane = lax.broadcasted_iota(jnp.int32, (1, 128), 1)
    wide = lax.broadcasted_iota(jnp.int32, (1, EX), 1)
    keep = kept_lanes(cross, n_xs)

    def shifted(prod):
        return jnp.where(wide == 0, 0.0, pltpu.roll(lines(prod, 3), 1, 1)) + jnp.where(
            wide == EX - 1, 0.0, pltpu.roll(lines(prod, 4), EX - 1, 1)
        )

    for s, k, prod, far, lanes in (
        (1, 1, near_b, far_b, slice(0, 128)), (10, 3, near_a, far_a, slice(128, 256)),
    ):
        coef = rim[2 * NODES : 3 * NODES] if s == 1 else rim[5 * NODES :]
        v_scr[at(s, 1), :EX] = (
            part[at(s, 1), :EX] + coef * h_scr[at(k), :] + lines(prod, 0) + far + shifted(prod)
            + cast(ends[2 * NODES : 3 * NODES, lanes], ends[3 * NODES :, lanes])
        )
    v_scr[at(2, 1), :EX] = part[at(2, 1), :EX] + lines(near_b, 1)
    v_scr[at(2, 1), EX:] = part[at(2, 1), EX:] + lines(ends, 0)[:, :128] * keep
    v_scr[at(9, 1), :EX] = part[at(9, 1), :EX] + lines(near_a, 2)
    v_scr[at(9, 1), EX:] = part[at(9, 1), EX:] + lines(ends, 1)[:, 128:] * keep
    v_scr[at(3, 1).start : at(8, 1).stop, :] = part[at(3, 1).start : at(8, 1).stop, :]

    casts = {}
    for s in range(2, 10, 2):
        pair = product(mats, jnp.concatenate([v_scr[at(s, 1), EX:], v_scr[at(s + 1, 1), EX:]], 1), 3, 5)
        casts[s] = cast(pair[:NODES, :128], pair[NODES:, :128])
        casts[s + 1] = cast(pair[:NODES, 128:], pair[NODES:, 128:])
    sums = [jnp.zeros((8, EX), f32) for _ in range(5)]
    low = product(mats, v_scr[at(1, 1), :EX], 1, 2)
    pending = None
    for s in range(2, 11):
        if s < 10:
            prod = product(mats, v_scr[at(s, 1), :EX], 0, 5)
            up = lines(prod, 2)
        else:
            up = product(mats, v_scr[at(s, 1), :EX], 2, 3)
        if pending is not None:
            r, v = r_own[at(s - 1, 2), :], v_scr[at(s - 1, 1), :EX]
            w = pending + up - THETA * v
            pairs = ((v, v), (v, w), (w, w), (r, v), (r, w))
            for k, (a, b) in enumerate(pairs):
                sums[k] = sums[k] + jnp.sum((a * b).reshape(8, 8, EX), axis=0)
        if s < 10:
            pending = (
                cf[at(s, 2), :] * v_scr[at(s, 1), :EX] + lines(prod, 0) + low + casts[s] + shifted(prod)
            )
            low = lines(prod, 1)

    gram = jnp.zeros((1, 128), f32)
    for k in range(5):
        total = jnp.sum(jnp.sum(sums[k], axis=0, keepdims=True), axis=1, keepdims=True)
        gram = gram + jnp.where(lane == k, total, 0.0)
    v_mid = v_scr[NODES : 9 * NODES, :EX]
    rows = [gram, tr[...], trace(v_mid, spot)]
    msg[...] = jnp.concatenate(rows * 128, 0)
    if not first:
        v_out[...] = v_mid


def solve(got):
    total = jnp.sum(got[pl.ds(0, 128, stride=3), :], axis=0, keepdims=True)
    lane = lax.broadcasted_iota(jnp.int32, (1, 128), 1)
    g11, g12, g22, g1, g2 = (
        jnp.sum(jnp.where(lane == k, total, 0.0), axis=1, keepdims=True) for k in range(5)
    )
    ratio = g12 / g11
    b = (g2 - ratio * g1) / (g22 - ratio * g12)
    a = (g1 - b * g12) / g11
    return a - THETA * b, b


def displace(a, b, got, compliance, disp, out):
    start = position()[0] * 48
    traces = a * got[pl.ds(start + 1, 16, stride=3), :] + b * got[pl.ds(start + 2, 16, stride=3), :]
    acc = jnp.zeros((IFN, 128), f32)
    for j in range(16):
        acc = acc + compliance[:, j * 128 : (j + 1) * 128] * traces[j : j + 1]
    fresh = jnp.sum(acc.T, axis=0, keepdims=True)
    out[...] = 0.5 * fresh + 0.5 * disp[...]


def shell_kernel(got, compliance, disp, out):
    displace(*solve(got), got, compliance, disp, out)


def final_kernel(got, compliance, disp, r, v, fluid, out):
    a, b = solve(got)
    displace(a, b, got, compliance, disp, out)
    for s in range(ES):
        field = a * r[at(s), :] + b * v[at(s), :]
        for h in (0, 1):
            fluid[pl.ds(h * ES + s, NODES, stride=2 * ES), :] = field[:, h * 128 : (h + 1) * 128]


def call(kernel, outs, ins, scratch=()):
    vm = pl.BlockSpec(memory_space=pltpu.VMEM)
    return pl.pallas_call(
        kernel,
        out_shape=[pltpu.VMEM(*o) for o in outs],
        in_specs=[vm] * len(ins),
        out_specs=[vm] * len(outs),
        scratch_shapes=[pltpu.VMEM(x, f32) for x in scratch],
        compiler_params=pltpu.CompilerParams(vmem_limit_bytes=16 << 20),
    )(*(pltpu.with_memory_space_constraint(x, pltpu.VMEM) for x in ins))


def swaps(axis, wrap):
    size = lax.axis_size(axis)
    pairs = [(i, i + 1) for i in range(size - 1)] + ([(size - 1, 0)] if wrap else [])
    return [[p for i, j in pairs[k::2] for p in ((i, j), (j, i))] for k in (0, 1)]


def body(
    source, coefficient, volume_matrix, span_lower, span_upper, cross_lower,
    cross_upper, interface, compliance, start_displacement,
):
    n_xs = lax.axis_size("xs")
    own, disp, rows = interface[0], start_displacement[0], compliance[0]
    mats = [volume_matrix, span_lower, span_upper, cross_lower, cross_upper]
    message, block = ((3 * 128, 128), f32), ((ES * NODES, EX), f32)
    row, wide = ((1, 128), f32), ((10 * NODES, LANES), f32)

    def trade(axis, a, b):
        first, second = swaps(axis, axis == "span")
        far = lax.ppermute(b, axis, second)
        near = lax.ppermute(a, axis, first)
        return [near, far]

    args = [x.reshape(ES * NODES, EX) for x in (source, coefficient)] + [own, disp] + mats
    far = pl.BlockSpec(memory_space=pl.ANY)
    packed, near_s, far_s, src, cf, own, disp, *mats = pl.pallas_call(
        pack,
        out_shape=[pltpu.VMEM((32, 128), f32)]
        + [pltpu.VMEM((3 * NODES, EX), f32)] * 2
        + [pltpu.VMEM(*block)] * 2
        + [pltpu.VMEM(x.shape, x.dtype) for x in args[2:]],
        in_specs=[far] * 9,
        out_specs=[pl.BlockSpec(memory_space=pltpu.VMEM)] * 12,
        scratch_shapes=[
            pltpu.VMEM((4, ES * NODES, 128), f32), pltpu.SemaphoreType.DMA((11,))
        ],
        compiler_params=pltpu.CompilerParams(vmem_limit_bytes=16 << 20),
        name="pack",
    )(*(pltpu.with_memory_space_constraint(x, pltpu.HBM) for x in args))
    ends = trade("span", near_s, far_s)
    cols = trade("xs", packed, packed)
    r, part, tr, split = call(
        lambda *refs: inner_kernel(True, *refs),
        [block, wide, row, ((5 * NODES, 3 * NODES), bf16)],
        [src, cf, own, disp, *mats],
    )
    small = call(pack_corner, [((8, 128), f32)] * 2, [*cols, own, disp])
    around = [*trade("span", *small), own]
    outers = ((ES * NODES, 128), f32)
    scratch = [(5 * NODES, EX), wide[0]]
    part, *cross = call(
        lambda *refs: side_kernel(True, n_xs, *refs), [wide, outers, outers],
        [part, split, *cols], [outers[0]],
    )
    sent, *static = call(
        lambda *refs: outer_kernel(True, n_xs, *refs),
        [message, ((6 * NODES, EX), f32), ((2 * NODES, 128), f32)],
        [cf, r, part, tr, split, *around, *ends], scratch,
    )
    got = lax.all_to_all(sent.reshape(128, 1, 384), AXES, 0, 0, tiled=True).reshape(384, 128)
    (disp,) = call(shell_kernel, [row], [got, rows, disp])
    beside = trade("xs", disp, disp)
    r, part, tr = call(
        lambda *refs: inner_kernel(False, *refs),
        [block, wide, row], [src, cf, own, disp, split],
    )
    (mid,) = call(join, [((3, 128), f32)], [*beside, disp])
    over = trade("span", mid, mid)
    (part,) = call(
        lambda *refs: side_kernel(False, n_xs, *refs), [wide],
        [part, split, *cols, *beside, *cross], [outers[0]],
    )
    sent, v = call(
        lambda *refs: outer_kernel(False, n_xs, *refs), [message, block],
        [cf, r, part, tr, split, *around, *over, *static], scratch,
    )
    got = lax.all_to_all(sent.reshape(128, 1, 384), AXES, 0, 0, tiled=True).reshape(384, 128)
    near = pl.BlockSpec(memory_space=pltpu.VMEM)
    fluid, disp = pl.pallas_call(
        final_kernel,
        out_shape=[jax.ShapeDtypeStruct((2 * ES * NODES, 128), f32), jax.ShapeDtypeStruct(*row)],
        in_specs=[near] * 5,
        out_specs=[near] * 2,
        compiler_params=pltpu.CompilerParams(vmem_limit_bytes=16 << 20),
        name="final",
    )(*(pltpu.with_memory_space_constraint(x, pltpu.VMEM) for x in (got, rows, disp, r, v)))
    fluid = fluid.reshape(NODES, 2, ES, 128).transpose(0, 2, 1, 3)
    return fluid.reshape(source.shape), disp[None]


def solution(mesh):
    field = P(None, "span", "xs")
    section = P("span", "xs", None)
    return jax.shard_map(
        body,
        mesh=mesh,
        in_specs=(field, field, P(), P(), P(), P(), P(), section, section, section),
        out_specs=(field, section),
        check_vma=False,
    )
```
